256 devices in a mesh: member: 4 (over y), seq: 64 (over z, x, core).
Axes of the slice: x: 4, y: 4, z: 8, core: 2. Of those that a mesh axis runs over, the one named last changes fastest.
Arguments:
- hidden: bfloat16 [4, 24576, 2880], P('member', 'seq'), may hold values from -6 to 6
- segments: int32 [24576], replicated, may hold values from 0 to 127, never falling along the last dimension, each value on 1 to 768 neighbouring positions
- pre_gain: float32 [4, 2880], P('member'), may hold values from 0.5 to 1.5
- w_query: bfloat16 [4, 2880, 2048], P('member', 'seq'), may hold values from -3 to 3
- w_key: bfloat16 [4, 2880, 256], P('member', 'seq'), may hold values from -3 to 3
- w_value: bfloat16 [4, 2880, 256], P('member', 'seq'), may hold values from -0.109375 to 0.109375
- w_output: bfloat16 [4, 2048, 2880], P('member', 'seq'), may hold values from -0.125 to 0.125
- post_gain: float32 [4, 2880], P('member'), may hold values from 0.5 to 1.5
- final_gain: float32 [4, 2880], P('member'), may hold values from 0.5 to 1.5
- w_judge: bfloat16 [4, 2880, 128], P('member'), may hold values from -0.21875 to 0.21875
Outputs:
- residual_out: bfloat16 [4, 24576, 2880], P('member', 'seq')
- logits: float32 [24576, 128], P('seq')
The draws below stay inside these ranges and needn't reach their ends.
Inputs may be any that keep to these rules, and one draw needn't show every extreme that they name: `segments`: segment numbers never fall from one token to the next; every number is used, each names 1 to 768 consecutive tokens, and one names exactly 768.
All inputs are finite; a program needn't handle non-finite values.
Results may differ from the reference program's by a relative error of at most 0.014.
Values may be sent and summed in bfloat16 or wider, within the bound.
A program may use at most 128 MiB of HBM per device.

```python
import math
import jax
import jax.numpy as jnp
import numpy as np
from jax import lax

D = 2880
QH = 32
KVH = 4
HD = 64
WINDOW = 128
JUDGE = 128
TOK_DEV = 384
MEMBERS = 4
TOKENS = 24576
SEGMENTS = 128


def loud_groups(key):
    chosen = jax.random.randint(jax.random.fold_in(key, 5), (MEMBERS,), 0, KVH)
    strength = jax.random.uniform(jax.random.fold_in(key, 6), (MEMBERS,), jnp.float32, 4.0, 6.0)
    return (chosen, strength)


def entries(key, shape):
    return jax.random.normal(key, shape, jnp.float32)


def projection_draw(key, salt, group_of):
    chosen, strength = loud_groups(key)
    loud = group_of[None, :] == chosen[:, None]
    factor = jnp.where(loud, strength[:, None], 1.0)
    base = entries(jax.random.fold_in(key, salt), (MEMBERS, D, group_of.shape[0]))
    values = base * (1.0 / math.sqrt(D)) * factor[:, None, :]
    return jnp.clip(values, -3.0, 3.0).astype(jnp.bfloat16)


def draw_w_query(key, part):
    group_of = jnp.arange(QH * HD, dtype=jnp.int32) // HD // (QH // KVH)
    return projection_draw(key, 11, group_of)


def draw_w_key(key, part):
    group_of = jnp.arange(KVH * HD, dtype=jnp.int32) // HD
    return projection_draw(key, 13, group_of)


def level_of(own_key, extent, pieces, low, high):
    gain = 1.0
    for position, shards_of in pieces:
        draws = jax.random.uniform(jax.random.fold_in(jax.random.fold_in(own_key, 6), position), (shards_of,), jnp.float32, low / len(pieces), high / len(pieces))
        gain = gain * jnp.repeat(jnp.exp(draws), extent[position] // shards_of).reshape((-1,) + (1,) * (len(extent) - 1 - position))
    return gain


def length_profile(count, total, reach, lean):
    portions = [(1 << 20) // math.isqrt(rank ** lean) + 1 for rank in range(2, count + 1)]
    spare, holding = total - reach - (count - 1), [1] * (count - 1)
    while spare > 0:
        movable = [i for i in range(count - 1) if holding[i] < reach]
        whole, left = sum([portions[i] for i in movable]), spare
        for i in movable:
            addition = min(reach - holding[i], max(1, left * portions[i] // whole), spare)
            holding[i] = holding[i] + addition
            spare = spare - addition
    return np.array([reach] + holding)


def uneven_parts(rng, number_of, total, reach, slope):
    if number_of == 2:
        one = jax.random.randint(rng, (), max(1, total - reach), min(reach, total - 1) + 1)
        return jnp.stack([one, total - one])
    lengths = jnp.asarray(length_profile(number_of, total, reach, slope), jnp.int32)
    couples = (number_of - 1) // 2
    giver, taker = lengths[1:1 + 2 * couples:2], lengths[2:2 + 2 * couples:2]
    slack = jnp.minimum(giver - 1, reach - taker)
    moved = jax.random.randint(jax.random.fold_in(rng, 1), (couples,), 0, 1 << 20) % (slack + 1)
    lengths = lengths.at[1:1 + 2 * couples:2].set(giver - moved).at[2:2 + 2 * couples:2].set(taker + moved)
    return lengths[jax.random.permutation(jax.random.fold_in(rng, 2), number_of)]


def normal_values(own_key, dims, spread, bound, split=(), kind=jnp.bfloat16):
    values = spread * jax.random.normal(own_key, dims, jnp.float32)
    if split:
        values = values * level_of(own_key, dims, split, -0.22, 0.18)
    return jnp.clip(values, -bound, bound).astype(kind)


def setup_inputs(seed: int = 0) -> dict:
    splits = jax.random.split(jax.random.key(seed), 11)
    hidden = normal_values(splits[0], (MEMBERS, TOKENS, D), 1.0, 6.0, ((0, 4), (1, 64)))
    segments = jnp.searchsorted(jnp.cumsum(uneven_parts(splits[1], SEGMENTS, TOKENS, 2 * TOK_DEV, 2)), jnp.arange(TOKENS), side="right").astype(jnp.int32)
    pre_gain = jnp.clip(0.5 + 1.0 * jax.random.uniform(splits[2], (MEMBERS, D), jnp.float32) ** level_of(splits[2], (MEMBERS, D), ((0, 4),), -0.2, 0.2), 0.5, 1.5)
    w_query = draw_w_query(jax.random.fold_in(splits[10], 71), 0)
    w_key = draw_w_key(jax.random.fold_in(splits[10], 71), 0)
    w_value = normal_values(splits[5], (MEMBERS, D, KVH * HD), D ** -0.5, 0.109375, ((0, 4), (1, 64)))
    w_output = normal_values(splits[6], (MEMBERS, QH * HD, D), (QH * HD) ** -0.5, 0.125, ((0, 4), (1, 64)))
    post_gain = jnp.clip(0.5 + 1.0 * jax.random.uniform(splits[7], (MEMBERS, D), jnp.float32) ** level_of(splits[7], (MEMBERS, D), ((0, 4),), -0.2, 0.2), 0.5, 1.5)
    final_gain = jnp.clip(0.5 + 1.0 * jax.random.uniform(splits[8], (MEMBERS, D), jnp.float32) ** level_of(splits[8], (MEMBERS, D), ((0, 4),), -0.2, 0.2), 0.5, 1.5)
    w_judge = normal_values(splits[9], (MEMBERS, D, JUDGE), (D // 4) ** -0.5, 0.21875, ((0, 4),))
    return {"hidden": hidden, "segments": segments, "pre_gain": pre_gain, "w_query": w_query, "w_key": w_key, "w_value": w_value, "w_output": w_output, "post_gain": post_gain, "final_gain": final_gain, "w_judge": w_judge}


epsilon = 1e-06
softcap = 50.0
rope_base = 10000.0

def rms_norm(inputs, scale_gain):
    values = inputs.astype(jnp.float32)
    return values * lax.rsqrt(lax.optimization_barrier(jnp.mean(values * values, axis=-1, keepdims=True)) + epsilon) * scale_gain

def rotate(inputs, positions):
    head_size = inputs.shape[-1]
    half_dim = head_size // 2
    frequency = jnp.exp(jnp.arange(half_dim, dtype=jnp.float32) * (-2.0 * math.log(rope_base) / head_size))
    angles = positions.astype(jnp.float32)[:, None] * frequency[None, :]
    cosine_term = jnp.cos(angles)[:, None, :]
    sine_term = jnp.sin(angles)[:, None, :]
    lower_half = inputs[..., :half_dim]
    upper_half = inputs[..., half_dim:]
    return jnp.concatenate([lower_half * cosine_term - upper_half * sine_term, upper_half * cosine_term + lower_half * sine_term], axis=-1)

def attend(queries, key_rows, val_rows, seg_query, seg_key):
    query_count = queries.shape[0]
    key_count = key_rows.shape[0]
    grouped = queries.reshape(query_count, KVH, QH // KVH, HD).astype(jnp.float32)
    key_heads = key_rows.reshape(key_count, KVH, HD).astype(jnp.float32)
    scores = jnp.einsum('qhgd,khd->hgqk', grouped, key_heads)
    scores = softcap * jnp.tanh(scores / softcap)
    distance = jnp.arange(query_count)[:, None] + (key_count - query_count) - jnp.arange(key_count)[None, :]
    allowed = (distance >= 0) & (distance < WINDOW) & (seg_query[:, None] == seg_key[None, :])
    expanded = jnp.where(allowed, jnp.exp(scores), 0.0)
    weights = (expanded / lax.optimization_barrier(jnp.sum(expanded, axis=-1, keepdims=True))).astype(jnp.bfloat16)
    value_heads = val_rows.reshape(key_count, KVH, HD).astype(jnp.float32)
    result = jnp.einsum('hgqk,khd->qhgd', weights.astype(jnp.float32), value_heads)
    return result.reshape(query_count, QH * HD).astype(jnp.bfloat16)

def member_pass(member_hidden, segments, pre_gain, w_query, w_key, w_value, w_output, post_gain, final_gain, w_judge):
    tok_count = member_hidden.shape[0]
    normed = rms_norm(member_hidden, pre_gain).astype(jnp.bfloat16)
    positions = jnp.arange(tok_count, dtype=jnp.int32)
    queries = jnp.dot(normed, w_query, preferred_element_type=jnp.float32).reshape(tok_count, QH, HD)
    queries = (rotate(queries, positions) * (1.0 / math.sqrt(HD))).astype(jnp.bfloat16).reshape(tok_count, QH * HD)
    key_rows = jnp.dot(normed, w_key, preferred_element_type=jnp.float32).reshape(tok_count, KVH, HD)
    key_rows = rotate(key_rows, positions).astype(jnp.bfloat16).reshape(tok_count, KVH * HD)
    val_rows = jnp.dot(normed, w_value, preferred_element_type=jnp.float32).astype(jnp.bfloat16)
    padded_keys = jnp.concatenate([jnp.zeros((WINDOW, KVH * HD), jnp.bfloat16), key_rows], axis=0)
    padded_values = jnp.concatenate([jnp.zeros((WINDOW, KVH * HD), jnp.bfloat16), val_rows], axis=0)
    padded_segments = jnp.concatenate([jnp.full((WINDOW,), -1, jnp.int32), segments.astype(jnp.int32)], axis=0)

    def one_block(block_number):
        row_start = (block_number * WINDOW).astype(jnp.int32)
        block_queries = lax.dynamic_slice_in_dim(queries, row_start, WINDOW, 0)
        block_keys = lax.dynamic_slice_in_dim(padded_keys, row_start, 2 * WINDOW, 0)
        block_values = lax.dynamic_slice_in_dim(padded_values, row_start, 2 * WINDOW, 0)
        seg_query = lax.dynamic_slice_in_dim(segments.astype(jnp.int32), row_start, WINDOW, 0)
        seg_key = lax.dynamic_slice_in_dim(padded_segments, row_start, 2 * WINDOW, 0)
        return attend(block_queries, block_keys, block_values, seg_query, seg_key)
    attended = lax.map(one_block, jnp.arange(tok_count // WINDOW, dtype=jnp.int32))
    attended = attended.reshape(tok_count, QH * HD)
    projected = jnp.dot(attended, w_output, preferred_element_type=jnp.float32)
    updated = (member_hidden.astype(jnp.float32) + rms_norm(projected, post_gain)).astype(jnp.bfloat16)
    closing = rms_norm(updated, final_gain).astype(jnp.bfloat16)
    verdict = jnp.dot(closing, w_judge, preferred_element_type=jnp.float32)
    return (updated, verdict)

def reference(hidden, segments, pre_gain, w_query, w_key, w_value, w_output, post_gain, final_gain, w_judge):
    member_count = hidden.shape[0]
    updated_all = []
    summed = jnp.zeros((hidden.shape[1], w_judge.shape[2]), jnp.float32)
    for member in range(member_count):
        updated, verdict = member_pass(hidden[member], segments, pre_gain[member], w_query[member], w_key[member], w_value[member], w_output[member], post_gain[member], final_gain[member], w_judge[member])
        updated_all.append(updated)
        summed = summed + verdict
    return (jnp.stack(updated_all, axis=0), summed / member_count)
```

```python
import math

import jax
import jax.numpy as jnp
from jax import lax
from jax.experimental import pallas as pl
from jax.experimental.pallas import tpu as pltpu
from jax.sharding import PartitionSpec as P

QH = 32
KVH = 4
HD = 64
WINDOW = 128
D = 2880
TOK = 384
XN = 4
ZN = 8
MEM = 4
BQ = 48
BO = 32
NQ = KVH * HD * 2 + QH * HD
CQ = 1024
CO = 1152

epsilon = 1e-06
softcap = 50.0
rope_base = 10000.0

f32 = jnp.float32
bf16 = jnp.bfloat16
MESH = pl.DeviceIdType.MESH


def mod(a, n):
    return lax.rem(a + n, n)


def kernel(
    hid,
    seg,
    pre_g,
    wqkv,
    wo,
    post_g,
    fin_g,
    wj,
    res_out,
    logit_out,
    WQ,
    WO,
    HID,
    SEG,
    PRE,
    POST,
    FIN,
    WJ,
    NRM,
    A,
    COS,
    SIN,
    Q,
    KV,
    HALO,
    KD,
    VD,
    ATT,
    PRJ,
    RES,
    VS,
    LOG,
    local_sem,
    qx,
    qz,
    qpz,
    qpx,
    ox,
    oz,
    opz,
    opx,
    d2d_recv,
    send_sem,
    halo_send,
    halo_recv,
    vs_send,
    vs_recv,
    out_sem,
):
    me = lax.axis_index("seq")
    mem = lax.axis_index("member")
    c = lax.rem(me, 2)
    x = lax.rem(me // 2, XN)
    z = me // (2 * XN)
    s = 1 - 2 * c

    def seq_of(zz, xx, cc):
        return (zz * XN + xx) * 2 + cc

    x_f = seq_of(z, mod(x + s, XN), c)
    x_b = seq_of(z, mod(x - s, XN), c)
    z_f = seq_of(mod(z + s, ZN), x, c)
    z_b = seq_of(mod(z - s, ZN), x, c)
    partner = seq_of(z, x, 1 - c)
    after = mod(me + 1, 64)
    before = mod(me - 1, 64)
    far = jnp.where(c == 0, before, after)

    def local(i, src, dst):
        return pltpu.make_async_copy(src, dst, local_sem.at[i])

    def own(buf, rows):
        return buf.at[pl.ds(pl.multiple_of(me * rows, rows), rows), :]

    loads = [
        local(0, wqkv, own(WQ, BQ)),
        local(1, wo, own(WO, BO)),
        local(2, hid, HID),
        local(3, pre_g, PRE),
        local(4, seg, SEG),
        local(5, post_g, POST),
        local(6, fin_g, FIN),
        local(7, wj, WJ),
    ]
    for load in loads:
        load.start()

    barrier = pltpu.get_barrier_semaphore()
    for peer in (x_f, x_b, z_f, z_b, partner, far):
        pl.semaphore_signal(barrier, inc=1, device_id={"seq": peer}, device_id_type=MESH)
    for delta in (1, 2, 3):
        pl.semaphore_signal(
            barrier, inc=1, device_id={"member": mod(mem + delta, MEM)}, device_id_type=MESH
        )
    pl.semaphore_wait(barrier, 9)

    def z_order(i):
        return mod(z + s * ((i + 1) // 2) * (1 - 2 * lax.rem(i, 2)), ZN)

    def x_order(i):
        return mod(x + s * ((i + 1) // 2) * (1 - 2 * lax.rem(i, 2)), XN)

    class Gather:
        def __init__(self, number, buf, rows, cut, rx, rz, pz, px):
            self.number, self.buf, self.rows, self.cut = number, buf, rows, cut
            self.width = buf.shape[1]
            self.rx, self.rz, self.pz, self.px = rx, rz, pz, px

        def block(self, part, zz, xx):
            first = pl.multiple_of(seq_of(zz, xx, c) * self.rows, self.rows)
            columns = pl.ds(0, self.cut) if part == 0 else pl.ds(self.cut, self.width - self.cut)
            return self.buf.at[pl.ds(first, self.rows), columns]

        def copy(self, part, zz, xx, recv, peer):
            ref = self.block(part, zz, xx)
            return pltpu.make_async_remote_copy(
                src_ref=ref,
                dst_ref=ref,
                send_sem=send_sem.at[self.number],
                recv_sem=recv,
                device_id={"seq": peer},
                device_id_type=MESH,
            )

        def send(self, part, zz, xx, recv, peer):
            self.copy(part, zz, xx, recv, peer).start()

        def wait(self, part, zz, xx, recv):
            self.copy(part, zz, xx, recv, partner).wait_recv()

        def share(self, part, zz, xx):
            self.send(part, zz, xx, d2d_recv.at[self.number], partner)

        def begin(self):
            self.send(0, z, x, self.rx.at[0], x_f)
            self.send(0, z, x, self.rx.at[1], x_b)
            self.send(1, z, x, self.pz.at[0], z_f)
            self.send(1, z, x, self.pz.at[1], z_b)
            self.send(1, z, x, self.px.at[0], x_f)
            self.send(1, z, x, self.px.at[16], x_b)
            self.send(0, z, x, self.rz.at[0], z_f)
            self.send(0, z, x, self.rz.at[16], z_b)
            self.share(0, z, x)
            self.share(1, z, x)

        def first(self, a):
            zz = z_order(a + 1)
            self.wait(1, zz, x, self.pz.at[a])

            @pl.when(a < 5)
            def _():
                onward = seq_of(mod(z + s * (1 - 2 * lax.rem(a, 2)), ZN), x, c)
                self.send(1, zz, x, self.pz.at[a + 2], onward)

            self.send(1, zz, x, self.px.at[a + 1], x_f)
            self.send(1, zz, x, self.px.at[a + 17], x_b)
            self.share(1, zz, x)

            @pl.when(a < 3)
            def _():
                xx = x_order(a + 1)
                self.wait(0, z, xx, self.rx.at[a])

                @pl.when(a == 0)
                def _():
                    self.send(0, z, xx, self.rx.at[2], x_f)

                self.send(0, z, xx, self.rz.at[a + 1], z_f)
                self.send(0, z, xx, self.rz.at[a + 17], z_b)
                self.share(0, z, xx)

        def second(self, r):
            zz = z_order(lax.rem(r, 8))
            xx = mod(x - s * (1 + r // 8), XN)
            self.wait(1, zz, xx, self.px.at[r])

            @pl.when(r < 8)
            def _():
                self.send(1, zz, xx, self.px.at[r + 8], x_f)

            self.share(1, zz, xx)
            xj = x_order(lax.rem(r, 4))
            zk = mod(z - s * (1 + r // 4), ZN)
            self.wait(0, zk, xj, self.rz.at[r])

            @pl.when(r < 12)
            def _():
                self.send(0, zk, xj, self.rz.at[r + 4], z_f)

            self.share(0, zk, xj)

            @pl.when(r < 8)
            def _():
                xb = mod(x + s, XN)
                self.wait(1, zz, xb, self.px.at[r + 16])
                self.share(1, zz, xb)

            @pl.when(r < 12)
            def _():
                zb = mod(z + s * (1 + r // 4), ZN)
                self.wait(0, zb, xj, self.rz.at[r + 16])

                @pl.when(r < 8)
                def _():
                    self.send(0, zb, xj, self.rz.at[r + 20], z_b)

                self.share(0, zb, xj)

        def finish(self):
            half = self.buf.at[pl.ds(0, 32 * self.rows), :]
            pltpu.make_async_copy(half, half, d2d_recv.at[self.number]).wait()

        def drain(self):
            sent = self.buf.at[pl.ds(0, 63 * self.rows), :]
            pltpu.make_async_copy(sent, sent, send_sem.at[self.number]).wait()

    gq = Gather(0, WQ, BQ, CQ, qx, qz, qpz, qpx)
    go = Gather(1, WO, BO, CO, ox, oz, opz, opx)

    loads[0].wait()
    gq.begin()

    loads[2].wait()
    loads[3].wait()
    NRM[:, pl.ds(2816, 128)] = jnp.zeros((TOK, 128), bf16)

    @pl.loop(0, 6)
    def _(i):
        rows = pl.ds(pl.multiple_of(i * 64, 64), 64)
        values = HID[rows, :].astype(f32)
        scale = lax.rsqrt(jnp.mean(values * values, axis=-1, keepdims=True) + epsilon)
        NRM[rows, pl.ds(0, D)] = (values * scale * PRE[...]).astype(bf16)

    @pl.loop(0, 8)
    def _(t):
        start = (t * 360) // 128 * 128
        lead = t * 360 - start
        column = lax.broadcasted_iota(jnp.int32, (1, 384), 1)
        group = jnp.zeros((1, 384), jnp.int32)
        for k in range(1, 8):
            group += jnp.where(column >= 48 * k, 1, 0)
        source = jnp.where(column - 48 * group < 45, column - 3 * group + lead, -1)
        pick = jnp.where(lax.broadcasted_iota(jnp.int32, (512, 384), 0) == source, 1.0, 0.0)
        window = NRM[:, pl.ds(pl.multiple_of(start, 128), 512)]
        moved = jnp.dot(window, pick.astype(bf16), preferred_element_type=f32)
        A[:, pl.ds(pl.multiple_of(t * 384, 384), 384)] = moved.astype(bf16)

        @pl.when(t < 7)
        def _():
            gq.first(t)

    lane = lax.broadcasted_iota(jnp.int32, (1, 128), 1)
    low_half = lax.rem(lane, 64) < 32
    first_head = lane < 64
    index = lax.rem(lane, 32).astype(f32)
    frequency = jnp.exp(index * (-2.0 * math.log(rope_base) / HD))
    sign = jnp.where(low_half, -1.0, 1.0)

    @pl.loop(0, 3)
    def _(i):
        rows = pl.ds(pl.multiple_of(i * 128, 128), 128)
        position = me * TOK + i * 128 + lax.broadcasted_iota(jnp.int32, (128, 128), 0)
        angle = position.astype(f32) * frequency
        COS[rows, :] = jnp.cos(angle)
        SIN[rows, :] = jnp.sin(angle) * sign

    @pl.loop(0, 10)
    def _(r):
        gq.second(r)

    loads[1].wait()
    go.begin()

    @pl.loop(10, 16)
    def _(r):
        gq.second(r)

    gq.finish()

    def rest(slot):
        @pl.when(slot < 7)
        def _():
            go.first(slot)

        @pl.when(slot >= 7)
        def _():
            go.second(slot - 7)

    def rotated(half):
        swapped = jnp.where(low_half, pltpu.roll(half, 96, 1), pltpu.roll(half, 32, 1))
        return half * COS[...] + swapped * SIN[...]

    def doubled(pair):
        turned = pltpu.roll(pair, 64, 1)
        return jnp.where(first_head, pair, turned), jnp.where(first_head, turned, pair)

    def project(tile):
        columns = pl.ds(pl.multiple_of(tile * 256, 256), 256)
        return jnp.dot(A[...], WQ[:, columns], preferred_element_type=f32)

    own_rows = pl.ds(WINDOW, TOK)
    keys = project(0)
    for p in range(2):
        pair = rotated(keys[:, 128 * p : 128 * p + 128]).astype(bf16)
        KV[:, pl.ds(128 * p, 128)] = pair
        for q, both in enumerate(doubled(pair.astype(f32))):
            KD[own_rows, pl.ds(128 * (2 * p + q), 128)] = both.astype(bf16)
    rest(0)
    vals = project(1)
    for p in range(2):
        pair = vals[:, 128 * p : 128 * p + 128].astype(bf16)
        KV[:, pl.ds(256 + 128 * p, 128)] = pair
        for q, both in enumerate(doubled(pair.astype(f32))):
            VD[own_rows, pl.ds(128 * (2 * p + q), 128)] = both.astype(bf16)
    rest(1)

    halo = pltpu.make_async_remote_copy(
        src_ref=KV.at[pl.ds(TOK - WINDOW, WINDOW), :],
        dst_ref=HALO,
        send_sem=halo_send,
        recv_sem=halo_recv,
        device_id={"seq": after},
        device_id_type=MESH,
    )

    def query_tile(i):
        tile = project(i + 2)
        for p in range(2):
            half = rotated(tile[:, 128 * p : 128 * p + 128]) * (1.0 / math.sqrt(HD))
            Q[:, pl.ds(pl.multiple_of(i * 256 + 128 * p, 128), 128)] = half.astype(bf16)
        rest(i + 2)

    @pl.loop(0, 1)
    def _(i):
        query_tile(i)

    halo.start()

    @pl.loop(1, 8)
    def _(i):
        query_tile(i)

    halo.wait()
    for p in range(2):
        for source, store in ((0, KD), (256, VD)):
            pair = HALO[:, pl.ds(source + 128 * p, 128)].astype(f32)
            for q, both in enumerate(doubled(pair)):
                store[pl.ds(0, WINDOW), pl.ds(128 * (2 * p + q), 128)] = both.astype(bf16)

    loads[4].wait()
    ones = jnp.ones((2 * WINDOW, 128), bf16)
    keep_a = jnp.where(first_head, 1.0, 0.0).astype(bf16)
    keep_b = jnp.where(first_head, 0.0, 1.0).astype(bf16)
    q_index = lax.broadcasted_iota(jnp.int32, (WINDOW, WINDOW), 0)
    k_index = lax.broadcasted_iota(jnp.int32, (WINDOW, WINDOW), 1)

    @pl.loop(0, 12)
    def _(i):
        block = i // 4
        head = lax.rem(i, 4)
        row = me * 3 + block
        seg_own = jnp.broadcast_to(SEG[pl.ds(row, 1), :], (WINDOW, WINDOW))
        seg_old = jnp.broadcast_to(SEG[pl.ds(jnp.maximum(row - 1, 0), 1), :], (WINDOW, WINDOW))
        seg_query = jnp.transpose(seg_own)
        old = (seg_query == seg_old) & (k_index > q_index) & (row > 0)
        new = (seg_query == seg_own) & (k_index <= q_index)
        allowed = jnp.concatenate(
            [jnp.where(old, 1.0, 0.0), jnp.where(new, 1.0, 0.0)], axis=1
        ).astype(bf16)
        allowed = jnp.concatenate([allowed, allowed], axis=0)
        q_rows = pl.ds(pl.multiple_of(block * 128, 128), 128)
        k_rows = pl.ds(pl.multiple_of(block * 128, 128), 256)
        k_cols = pl.ds(pl.multiple_of(head * 128, 128), 128)
        kd = KD[k_rows, k_cols]
        vd = jnp.concatenate([VD[k_rows, k_cols], ones], axis=1)
        for p in range(4):
            cols = pl.ds(pl.multiple_of(head * 512 + 128 * p, 128), 128)
            pair = Q[q_rows, cols]
            stacked = jnp.concatenate([pair * keep_a, pair * keep_b], axis=0)
            scores = lax.dot_general(
                stacked, kd, (((1,), (1,)), ((), ())), preferred_element_type=f32
            )
            weights = jnp.exp(softcap * jnp.tanh(scores * (1.0 / softcap))).astype(bf16) * allowed
            mixed = jnp.dot(weights, vd, preferred_element_type=f32)
            mixed = mixed[:, :128] / mixed[:, 128:]
            ATT[q_rows, cols] = jnp.where(first_head, mixed[:128], mixed[128:]).astype(bf16)
        rest(i + 10)

    rest(22)
    go.finish()

    @pl.loop(0, 11)
    def _(i):
        columns = pl.ds(pl.multiple_of(i * 256, 256), 256)
        PRJ[:, columns] = jnp.dot(ATT[...], WO[:, columns], preferred_element_type=f32)

    PRJ[:, pl.ds(2816, 64)] = jnp.dot(ATT[...], WO[:, pl.ds(2816, 64)], preferred_element_type=f32)

    for load in loads[5:]:
        load.wait()

    def verdict_copy(delta, block):
        rows = pl.ds(pl.multiple_of(block * 128, 128), 128)
        ref = VS.at[mem, rows, :]
        return pltpu.make_async_remote_copy(
            src_ref=ref,
            dst_ref=ref,
            send_sem=vs_send,
            recv_sem=vs_recv.at[(delta - 1) * 3 + block],
            device_id={"member": mod(mem + delta, MEM)},
            device_id_type=MESH,
        )

    def res_copy(block):
        rows = pl.ds(pl.multiple_of(block * 128, 128), 128)
        return pltpu.make_async_copy(RES.at[rows, :], res_out.at[rows, :], out_sem.at[block])

    def issue(block):
        res_copy(block).start()
        for delta in (1, 2, 3):
            verdict_copy(delta, block).start()

    @pl.loop(0, 3)
    def _(i):
        for h in range(2):
            rows = pl.ds(pl.multiple_of(i * 128 + 64 * h, 64), 64)
            projected = PRJ[rows, :]
            scale = lax.rsqrt(jnp.mean(projected * projected, axis=-1, keepdims=True) + epsilon)
            updated = (HID[rows, :].astype(f32) + projected * scale * POST[...]).astype(bf16)
            RES[rows, :] = updated
            values = updated.astype(f32)
            scale = lax.rsqrt(jnp.mean(values * values, axis=-1, keepdims=True) + epsilon)
            closing = (values * scale * FIN[...]).astype(bf16)
            verdict = jnp.dot(closing, WJ[...], preferred_element_type=f32)
            VS[mem, rows, :] = verdict.astype(bf16)

        @pl.when(i > 0)
        def _():
            issue(i - 1)

    gq.drain()
    go.drain()
    issue(2)
    for block in range(3):
        for delta in (1, 2, 3):
            verdict_copy(delta, block).wait_recv()
        rows = pl.ds(block * 128, 128)
        total = VS[0, rows, :].astype(f32) + VS[1, rows, :].astype(f32)
        total = total + VS[2, rows, :].astype(f32) + VS[3, rows, :].astype(f32)
        LOG[rows, :] = total * 0.25
    done = pltpu.make_async_copy(LOG, logit_out, out_sem.at[3])
    done.start()
    sent = WO.at[pl.ds(0, 9 * 128), pl.ds(0, 128)]
    pltpu.make_async_copy(sent, sent, vs_send).wait()
    for block in range(3):
        res_copy(block).wait()
    done.wait()


def body(
    hidden, segments, pre_gain, w_query, w_key, w_value, w_output, post_gain, final_gain, w_judge
):
    wqkv = jnp.pad(jnp.concatenate([w_key[0], w_value[0], w_query[0]], axis=1), ((0, 3), (0, 0)))
    dma = pltpu.SemaphoreType.DMA
    any_spec = pl.BlockSpec(memory_space=pl.ANY)
    gather_sems = [dma((3,)), dma((28,)), dma((7,)), dma((24,))]
    updated, logits = pl.pallas_call(
        kernel,
        out_shape=(
            jax.ShapeDtypeStruct((TOK, D), bf16),
            jax.ShapeDtypeStruct((TOK, 128), f32),
        ),
        in_specs=[any_spec] * 8,
        out_specs=(any_spec, any_spec),
        scratch_shapes=[
            pltpu.VMEM((64 * BQ, NQ), bf16),
            pltpu.VMEM((64 * BO, D), bf16),
            pltpu.VMEM((TOK, D), bf16),
            pltpu.VMEM((192, 128), jnp.int32),
            pltpu.VMEM((1, D), f32),
            pltpu.VMEM((1, D), f32),
            pltpu.VMEM((1, D), f32),
            pltpu.VMEM((D, 128), bf16),
            pltpu.VMEM((TOK, 2944), bf16),
            pltpu.VMEM((TOK, 64 * BQ), bf16),
            pltpu.VMEM((TOK, 128), f32),
            pltpu.VMEM((TOK, 128), f32),
            pltpu.VMEM((TOK, QH * HD), bf16),
            pltpu.VMEM((TOK, 512), bf16),
            pltpu.VMEM((WINDOW, 512), bf16),
            pltpu.VMEM((WINDOW + TOK, 512), bf16),
            pltpu.VMEM((WINDOW + TOK, 512), bf16),
            pltpu.VMEM((TOK, QH * HD), bf16),
            pltpu.VMEM((TOK, D), f32),
            pltpu.VMEM((TOK, D), bf16),
            pltpu.VMEM((MEM, TOK, 128), bf16),
            pltpu.VMEM((TOK, 128), f32),
            dma((8,)),
            *gather_sems,
            *gather_sems,
            dma((2,)),
            dma((2,)),
            dma,
            dma,
            dma,
            dma((9,)),
            dma((4,)),
        ],
        compiler_params=pltpu.CompilerParams(
            collective_id=0, has_side_effects=True, vmem_limit_bytes=62 * 1024 * 1024
        ),
    )(
        hidden[0],
        segments.reshape(192, 128),
        pre_gain,
        wqkv,
        w_output[0],
        post_gain,
        final_gain,
        w_judge[0],
    )
    return updated[None], logits


def solution(mesh):
    return jax.shard_map(
        body,
        mesh=mesh,
        in_specs=(
            P("member", "seq", None),
            P(),
            P("member", None),
            P("member", "seq", None),
            P("member", "seq", None),
            P("member", "seq", None),
            P("member", "seq", None),
            P("member", None),
            P("member", None),
            P("member", None, None),
        ),
        out_specs=(P("member", "seq", None), P("seq", None)),
        check_vma=False,
    )
```

```python
import math

import jax
import jax.numpy as jnp
from jax import lax
from jax.experimental import pallas as pl
from jax.experimental.pallas import tpu as pltpu
from jax.sharding import PartitionSpec as P

QH = 32
KVH = 4
HD = 64
WINDOW = 128
D = 2880
TOK = 384
XN = 4
ZN = 8
MEM = 4
BQ = 48
BO = 32
NQ = KVH * HD * 2 + QH * HD
CQ = 1024
CO = 1152

epsilon = 1e-06
softcap = 50.0
rope_base = 10000.0

f32 = jnp.float32
bf16 = jnp.bfloat16
MESH = pl.DeviceIdType.MESH


def mod(a, n):
    return lax.rem(a + n, n)


def kernel(
    hid,
    seg,
    pre_g,
    wq,
    wk,
    wv,
    wo,
    post_g,
    fin_g,
    wj,
    RT,
    LOG,
    WQ,
    WOX,
    WOZ,
    SQ,
    SK,
    SV,
    HT,
    HID,
    SEG,
    PRE,
    POST,
    FIN,
    WJ,
    NRM,
    A,
    COS,
    SIN,
    Q,
    KV,
    HALO,
    KD,
    VD,
    ATT,
    ATTZ,
    PRJ,
    VS,
    local_sem,
    qx,
    qz,
    qpz,
    qpx,
    ox,
    oz,
    opz,
    opx,
    q_shared,
    ox_shared,
    oz_shared,
    send_sem,
    halo_send,
    halo_recv,
    vs_send,
    vs_recv,
):
    me = lax.axis_index("seq")
    mem = lax.axis_index("member")
    c = lax.rem(me, 2)
    x = lax.rem(me // 2, XN)
    z = me // (2 * XN)
    s = 1 - 2 * c

    def seq_of(zz, xx, cc):
        return (zz * XN + xx) * 2 + cc

    x_f = seq_of(z, mod(x + s, XN), c)
    x_b = seq_of(z, mod(x - s, XN), c)
    z_f = seq_of(mod(z + s, ZN), x, c)
    z_b = seq_of(mod(z - s, ZN), x, c)
    partner = seq_of(z, x, 1 - c)
    after = mod(me + 1, 64)
    before = mod(me - 1, 64)
    far = jnp.where(c == 0, before, after)

    def local(i, src, dst):
        return pltpu.make_async_copy(src, dst, local_sem.at[i])

    own_x = pl.ds(pl.multiple_of(me * BO, BO), BO)
    own_z = pl.ds(pl.multiple_of(((x * ZN + z) * 2 + c) * BO, BO), BO)
    loads = [
        local(0, wk, SK),
        local(1, wv, SV),
        local(2, wq, SQ),
        local(3, hid, HT),
        local(4, wo.at[:, pl.ds(0, CO)], WOX.at[own_x, :]),
        local(5, wo.at[:, pl.ds(CO, D - CO)], WOZ.at[own_z, :]),
        local(6, pre_g, PRE),
        local(7, seg, SEG),
        local(8, post_g, POST),
        local(9, fin_g, FIN),
        local(10, wj, WJ),
    ]
    for load in loads:
        load.start()

    barrier = pltpu.get_barrier_semaphore()
    for peer in (x_f, x_b, z_f, z_b, partner, far):
        pl.semaphore_signal(barrier, inc=1, device_id={"seq": peer}, device_id_type=MESH)
    for delta in (1, 2, 3):
        pl.semaphore_signal(
            barrier, inc=1, device_id={"member": mod(mem + delta, MEM)}, device_id_type=MESH
        )
    own_q = pl.ds(pl.multiple_of(me * BQ, BQ), BQ)
    for load, stage, first, width in ((0, SK, 0, 256), (1, SV, 256, 256), (2, SQ, 512, 2048)):
        loads[load].wait()
        padded = jnp.concatenate([stage[...], jnp.zeros((3, width), bf16)], axis=0)
        WQ[own_q, pl.ds(first, width)] = padded
    pl.semaphore_wait(barrier, 9)

    def z_order(i):
        return mod(z + s * ((i + 1) // 2) * (1 - 2 * lax.rem(i, 2)), ZN)

    def x_order(i):
        return mod(x + s * ((i + 1) // 2) * (1 - 2 * lax.rem(i, 2)), XN)

    class Gather:
        def __init__(self, number, rows, bufs, shared, rx, rz, pz, px):
            self.number, self.rows, self.bufs, self.shared = number, rows, bufs, shared
            self.rx, self.rz, self.pz, self.px = rx, rz, pz, px

        def block(self, part, zz, xx):
            buf, columns, z_major = self.bufs[part]
            place = seq_of(zz, xx, c) if z_major else (xx * ZN + zz) * 2 + c
            return buf.at[pl.ds(pl.multiple_of(place * self.rows, self.rows), self.rows), columns]

        def copy(self, part, zz, xx, recv, peer):
            ref = self.block(part, zz, xx)
            return pltpu.make_async_remote_copy(
                src_ref=ref,
                dst_ref=ref,
                send_sem=send_sem.at[self.number + part],
                recv_sem=recv,
                device_id={"seq": peer},
                device_id_type=MESH,
            )

        def send(self, part, zz, xx, recv, peer):
            self.copy(part, zz, xx, recv, peer).start()

        def wait(self, part, zz, xx, recv):
            self.copy(part, zz, xx, recv, partner).wait_recv()

        def share(self, part, zz, xx):
            self.send(part, zz, xx, self.shared[part](zz, xx), partner)

        def begin(self):
            self.send(0, z, x, self.rx.at[0], x_f)
            self.send(0, z, x, self.rx.at[1], x_b)
            self.send(1, z, x, self.pz.at[0], z_f)
            self.send(1, z, x, self.pz.at[1], z_b)
            self.send(1, z, x, self.px.at[0], x_f)
            self.send(1, z, x, self.px.at[16], x_b)
            self.send(0, z, x, self.rz.at[0], z_f)
            self.send(0, z, x, self.rz.at[16], z_b)
            self.share(0, z, x)
            self.share(1, z, x)

        def first(self, a):
            zz = z_order(a + 1)
            self.wait(1, zz, x, self.pz.at[a])

            @pl.when(a < 5)
            def _():
                onward = seq_of(mod(z + s * (1 - 2 * lax.rem(a, 2)), ZN), x, c)
                self.send(1, zz, x, self.pz.at[a + 2], onward)

            self.send(1, zz, x, self.px.at[a + 1], x_f)
            self.send(1, zz, x, self.px.at[a + 17], x_b)
            self.share(1, zz, x)

            @pl.when(a < 3)
            def _():
                xx = x_order(a + 1)
                self.wait(0, z, xx, self.rx.at[a])

                @pl.when(a == 0)
                def _():
                    self.send(0, z, xx, self.rx.at[2], x_f)

                self.send(0, z, xx, self.rz.at[a + 1], z_f)
                self.send(0, z, xx, self.rz.at[a + 17], z_b)
                self.share(0, z, xx)

        def second(self, r):
            zz = z_order(lax.rem(r, 8))
            xx = mod(x - s * (1 + r // 8), XN)
            self.wait(1, zz, xx, self.px.at[r])

            @pl.when(r < 8)
            def _():
                self.send(1, zz, xx, self.px.at[r + 8], x_f)

            self.share(1, zz, xx)
            xj = x_order(lax.rem(r, 4))
            zk = mod(z - s * (1 + r // 4), ZN)
            self.wait(0, zk, xj, self.rz.at[r])

            @pl.when(r < 12)
            def _():
                self.send(0, zk, xj, self.rz.at[r + 4], z_f)

            self.share(0, zk, xj)

            @pl.when(r < 8)
            def _():
                xb = mod(x + s, XN)
                self.wait(1, zz, xb, self.px.at[r + 16])
                self.share(1, zz, xb)

            @pl.when(r < 12)
            def _():
                zb = mod(z + s * (1 + r // 4), ZN)
                self.wait(0, zb, xj, self.rz.at[r + 16])

                @pl.when(r < 8)
                def _():
                    self.send(0, zb, xj, self.rz.at[r + 20], z_b)

                self.share(0, zb, xj)

        def drain(self):
            for part in range(2):
                buf, columns, _ = self.bufs[part]
                sent = buf.at[pl.ds(0, 63 * self.rows), columns]
                pltpu.make_async_copy(sent, sent, send_sem.at[self.number + part]).wait()

    def arrived(sem, ref):
        pltpu.make_async_copy(ref, ref, sem).wait()

    gq = Gather(
        0,
        BQ,
        ((WQ, pl.ds(0, CQ), True), (WQ, pl.ds(CQ, NQ - CQ), True)),
        (lambda zz, xx: q_shared.at[0], lambda zz, xx: q_shared.at[0]),
        qx,
        qz,
        qpz,
        qpx,
    )
    go = Gather(
        2,
        BO,
        ((WOX, slice(None), True), (WOZ, slice(None), False)),
        (lambda zz, xx: ox_shared.at[zz], lambda zz, xx: oz_shared.at[xx]),
        ox,
        oz,
        opz,
        opx,
    )

    gq.begin()

    lane = lax.broadcasted_iota(jnp.int32, (1, 128), 1)
    low_half = lax.rem(lane, 64) < 32
    first_head = lane < 64
    index = lax.rem(lane, 32).astype(f32)
    frequency = jnp.exp(index * (-2.0 * math.log(rope_base) / HD))
    sign = jnp.where(low_half, -1.0, 1.0)

    @pl.loop(0, 3)
    def _(i):
        rows = pl.ds(pl.multiple_of(i * 128, 128), 128)
        position = me * TOK + i * 128 + lax.broadcasted_iota(jnp.int32, (128, 128), 0)
        angle = position.astype(f32) * frequency
        COS[rows, :] = jnp.cos(angle)
        SIN[rows, :] = jnp.sin(angle) * sign

    loads[3].wait()

    @pl.loop(0, 7)
    def _(i):
        for k in range(3):
            features = pl.ds(pl.multiple_of(i * 384 + k * 128, 128), 128)
            HID[:, features] = jnp.transpose(HT[features, :])
        gq.first(i)

    HID[:, pl.ds(2688, 128)] = jnp.transpose(HT[pl.ds(2688, 128), :])
    HID[:, pl.ds(2816, 64)] = jnp.transpose(HT[pl.ds(2816, 64), :])

    loads[6].wait()
    NRM[:, pl.ds(2816, 128)] = jnp.zeros((TOK, 128), bf16)

    @pl.loop(0, 6)
    def _(i):
        rows = pl.ds(pl.multiple_of(i * 64, 64), 64)
        values = HID[rows, :].astype(f32)
        scale = lax.rsqrt(jnp.mean(values * values, axis=-1, keepdims=True) + epsilon)
        NRM[rows, pl.ds(0, D)] = (values * scale * PRE[...]).astype(bf16)
        PRJ[rows, :] = jnp.zeros((64, D), f32)
        gq.second(i)

    @pl.loop(0, 8)
    def _(t):
        start = (t * 360) // 128 * 128
        lead = t * 360 - start
        column = lax.broadcasted_iota(jnp.int32, (1, 384), 1)
        group = jnp.zeros((1, 384), jnp.int32)
        for k in range(1, 8):
            group += jnp.where(column >= 48 * k, 1, 0)
        source = jnp.where(column - 48 * group < 45, column - 3 * group + lead, -1)
        pick = jnp.where(lax.broadcasted_iota(jnp.int32, (512, 384), 0) == source, 1.0, 0.0)
        window = NRM[:, pl.ds(pl.multiple_of(start, 128), 512)]
        moved = jnp.dot(window, pick.astype(bf16), preferred_element_type=f32)
        A[:, pl.ds(pl.multiple_of(t * 384, 384), 384)] = moved.astype(bf16)
        gq.second(t + 6)

    loads[4].wait()
    loads[5].wait()
    go.begin()

    @pl.loop(14, 16)
    def _(r):
        gq.second(r)

    arrived(q_shared.at[0], WQ.at[pl.ds(0, 32 * BQ), :])

    def rotated(half):
        swapped = jnp.where(low_half, pltpu.roll(half, 96, 1), pltpu.roll(half, 32, 1))
        return half * COS[...] + swapped * SIN[...]

    def doubled(pair):
        turned = pltpu.roll(pair, 64, 1)
        return jnp.where(first_head, pair, turned), jnp.where(first_head, turned, pair)

    def project(tile):
        columns = pl.ds(pl.multiple_of(tile * 256, 256), 256)
        return jnp.dot(A[...], WQ[:, columns], preferred_element_type=f32)

    own_rows = pl.ds(WINDOW, TOK)
    keys = project(0)
    for p in range(2):
        pair = rotated(keys[:, 128 * p : 128 * p + 128]).astype(bf16)
        KV[:, pl.ds(128 * p, 128)] = pair
        for q, both in enumerate(doubled(pair.astype(f32))):
            KD[own_rows, pl.ds(128 * (2 * p + q), 128)] = both.astype(bf16)
    vals = project(1)
    for p in range(2):
        pair = vals[:, 128 * p : 128 * p + 128].astype(bf16)
        KV[:, pl.ds(256 + 128 * p, 128)] = pair
        for q, both in enumerate(doubled(pair.astype(f32))):
            VD[own_rows, pl.ds(128 * (2 * p + q), 128)] = both.astype(bf16)
    go.first(0)

    halo = pltpu.make_async_remote_copy(
        src_ref=KV.at[pl.ds(TOK - WINDOW, WINDOW), :],
        dst_ref=HALO,
        send_sem=halo_send,
        recv_sem=halo_recv,
        device_id={"seq": after},
        device_id_type=MESH,
    )

    def query_tile(i):
        tile = project(i + 2)
        for p in range(2):
            half = rotated(tile[:, 128 * p : 128 * p + 128]) * (1.0 / math.sqrt(HD))
            Q[:, pl.ds(pl.multiple_of(i * 256 + 128 * p, 128), 128)] = half.astype(bf16)

        @pl.when((i == 2) | (i == 5))
        def _():
            go.first((i + 1) // 3)

    @pl.loop(0, 1)
    def _(i):
        query_tile(i)

    halo.start()

    @pl.loop(1, 8)
    def _(i):
        query_tile(i)

    halo.wait()
    for p in range(2):
        for source, store in ((0, KD), (256, VD)):
            pair = HALO[:, pl.ds(source + 128 * p, 128)].astype(f32)
            for q, both in enumerate(doubled(pair)):
                store[pl.ds(0, WINDOW), pl.ds(128 * (2 * p + q), 128)] = both.astype(bf16)

    loads[7].wait()
    ones = jnp.ones((2 * WINDOW, 128), bf16)
    keep_a = jnp.where(first_head, 1.0, 0.0).astype(bf16)
    keep_b = jnp.where(first_head, 0.0, 1.0).astype(bf16)
    q_index = lax.broadcasted_iota(jnp.int32, (WINDOW, WINDOW), 0)
    k_index = lax.broadcasted_iota(jnp.int32, (WINDOW, WINDOW), 1)

    @pl.loop(0, 12)
    def _(i):
        block = i // 4
        head = lax.rem(i, 4)
        row = me * 3 + block
        seg_own = jnp.broadcast_to(SEG[pl.ds(row, 1), :], (WINDOW, WINDOW))
        seg_old = jnp.broadcast_to(SEG[pl.ds(jnp.maximum(row - 1, 0), 1), :], (WINDOW, WINDOW))
        seg_query = jnp.transpose(seg_own)
        old = (seg_query == seg_old) & (k_index > q_index) & (row > 0)
        new = (seg_query == seg_own) & (k_index <= q_index)
        allowed = jnp.concatenate(
            [jnp.where(old, 1.0, 0.0), jnp.where(new, 1.0, 0.0)], axis=1
        ).astype(bf16)
        allowed = jnp.concatenate([allowed, allowed], axis=0)
        q_rows = pl.ds(pl.multiple_of(block * 128, 128), 128)
        k_rows = pl.ds(pl.multiple_of(block * 128, 128), 256)
        k_cols = pl.ds(pl.multiple_of(head * 128, 128), 128)
        kd = KD[k_rows, k_cols]
        vd = jnp.concatenate([VD[k_rows, k_cols], ones], axis=1)
        mixed = []
        for p in range(4):
            cols = pl.ds(pl.multiple_of(head * 512 + 128 * p, 128), 128)
            pair = Q[q_rows, cols]
            stacked = jnp.concatenate([pair * keep_a, pair * keep_b], axis=0)
            scores = lax.dot_general(
                stacked, kd, (((1,), (1,)), ((), ())), preferred_element_type=f32
            )
            weights = jnp.exp(softcap * jnp.tanh(scores * (1.0 / softcap))).astype(bf16) * allowed
            both = jnp.dot(weights, vd, preferred_element_type=f32)
            both = (both[:, :128] / both[:, 128:]).astype(bf16)
            mixed += [both[:128], both[128:]]
            ATT[q_rows, cols] = jnp.where(first_head, mixed[2 * p], mixed[2 * p + 1])
        for k in range(4):
            cols = pl.ds(pl.multiple_of(k * 512 + head * 128, 128), 128)
            ATTZ[q_rows, cols] = jnp.where(first_head, mixed[k], mixed[k + 4])

        @pl.when(lax.rem(i, 3) == 2)
        def _():
            go.first(i // 3 + 3)

    def add_z_unit(zz):
        rows = pl.ds(pl.multiple_of(zz * 256, 256), 256)
        arrived(ox_shared.at[zz], WOX.at[pl.ds(0, 4 * BO), :])
        PRJ[:, pl.ds(0, CO)] += jnp.dot(ATT[:, rows], WOX[rows, :], preferred_element_type=f32)

    def add_x_unit(xx):
        rows = pl.ds(pl.multiple_of(xx * 512, 512), 512)
        arrived(oz_shared.at[xx], WOZ.at[pl.ds(0, 8 * BO), :])
        PRJ[:, pl.ds(CO, D - CO)] += jnp.dot(
            ATTZ[:, rows], WOZ[rows, :], preferred_element_type=f32
        )

    @pl.loop(0, 16)
    def _(r):
        go.second(r)

        @pl.when((r == 1) | ((r >= 5) & (r < 9)) | (r == 13) | (r == 14))
        def _():
            add_z_unit(z_order(jnp.where(r == 1, 0, jnp.where(r < 9, r - 4, r - 8))))

        @pl.when((r == 0) | (r == 9) | (r == 10))
        def _():
            add_x_unit(x_order(jnp.where(r == 0, 0, r - 8)))

    add_z_unit(z_order(7))
    add_x_unit(x_order(3))

    for load in loads[8:]:
        load.wait()

    def verdict_copy(delta, block):
        rows = pl.ds(pl.multiple_of(block * 128, 128), 128)
        ref = VS.at[mem, rows, :]
        return pltpu.make_async_remote_copy(
            src_ref=ref,
            dst_ref=ref,
            send_sem=vs_send,
            recv_sem=vs_recv.at[(delta - 1) * 3 + block],
            device_id={"member": mod(mem + delta, MEM)},
            device_id_type=MESH,
        )

    def turn(block, first, count):
        tokens = pl.ds(pl.multiple_of(block * 128, 128), 128)
        for k in range(first, first + count):
            features = pl.ds(128 * k, 128 if k < 22 else 64)
            RT[features, tokens] = jnp.transpose(NRM[tokens, features])

    @pl.loop(0, 3)
    def _(i):
        for h in range(2):
            rows = pl.ds(pl.multiple_of(i * 128 + 64 * h, 64), 64)
            projected = PRJ[rows, :]
            scale = lax.rsqrt(jnp.mean(projected * projected, axis=-1, keepdims=True) + epsilon)
            updated = (HID[rows, :].astype(f32) + projected * scale * POST[...]).astype(bf16)
            NRM[rows, pl.ds(0, D)] = updated
            values = updated.astype(f32)
            scale = lax.rsqrt(jnp.mean(values * values, axis=-1, keepdims=True) + epsilon)
            closing = (values * scale * FIN[...]).astype(bf16)
            verdict = jnp.dot(closing, WJ[...], preferred_element_type=f32)
            VS[mem, rows, :] = verdict.astype(bf16)
        turn(i, 0, 8)
        for delta in (2, 1, 3):
            verdict_copy(delta, i).start()
        turn(i, 8, 15)

    gq.drain()
    go.drain()
    for block in range(3):
        for delta in (1, 2, 3):
            verdict_copy(delta, block).wait_recv()
        rows = pl.ds(block * 128, 128)
        total = VS[0, rows, :].astype(f32) + VS[1, rows, :].astype(f32)
        total = total + VS[2, rows, :].astype(f32) + VS[3, rows, :].astype(f32)
        LOG[rows, :] = total * 0.25
    sent = WQ.at[pl.ds(0, 9 * 128), pl.ds(0, 128)]
    arrived(vs_send, sent)


def body(
    hidden, segments, pre_gain, w_query, w_key, w_value, w_output, post_gain, final_gain, w_judge
):
    dma = pltpu.SemaphoreType.DMA
    vmem = pltpu.VMEM
    any_spec = pl.BlockSpec(memory_space=pl.ANY)
    vmem_spec = pl.BlockSpec(memory_space=pltpu.VMEM)
    gather_sems = [dma((3,)), dma((28,)), dma((7,)), dma((24,))]
    updated, logits = pl.pallas_call(
        kernel,
        out_shape=(
            vmem((D, TOK), bf16),
            vmem((TOK, 128), f32),
        ),
        in_specs=[any_spec] * 10,
        out_specs=(vmem_spec, vmem_spec),
        scratch_shapes=[
            vmem((64 * BQ, NQ), bf16),
            vmem((64 * BO, CO), bf16),
            vmem((64 * BO, D - CO), bf16),
            vmem((45, 2048), bf16),
            vmem((45, 256), bf16),
            vmem((45, 256), bf16),
            vmem((D, TOK), bf16),
            vmem((TOK, D), bf16),
            vmem((192, 128), jnp.int32),
            vmem((1, D), f32),
            vmem((1, D), f32),
            vmem((1, D), f32),
            vmem((D, 128), bf16),
            vmem((TOK, 2944), bf16),
            vmem((TOK, 64 * BQ), bf16),
            vmem((TOK, 128), f32),
            vmem((TOK, 128), f32),
            vmem((TOK, QH * HD), bf16),
            vmem((TOK, 512), bf16),
            vmem((WINDOW, 512), bf16),
            vmem((WINDOW + TOK, 512), bf16),
            vmem((WINDOW + TOK, 512), bf16),
            vmem((TOK, QH * HD), bf16),
            vmem((TOK, QH * HD), bf16),
            vmem((TOK, D), f32),
            vmem((MEM, TOK, 128), bf16),
            dma((11,)),
            *gather_sems,
            *gather_sems,
            dma((1,)),
            dma((ZN,)),
            dma((XN,)),
            dma((4,)),
            dma,
            dma,
            dma,
            dma((9,)),
        ],
        compiler_params=pltpu.CompilerParams(
            collective_id=0, has_side_effects=True, vmem_limit_bytes=60 * 1024 * 1024
        ),
    )(
        hidden[0].T,
        segments.reshape(192, 128),
        pre_gain,
        w_query[0],
        w_key[0],
        w_value[0],
        w_output[0],
        post_gain,
        final_gain,
        w_judge[0],
    )
    return updated.T[None], logits


def solution(mesh):
    return jax.shard_map(
        body,
        mesh=mesh,
        in_specs=(
            P("member", "seq", None),
            P(),
            P("member", None),
            P("member", "seq", None),
            P("member", "seq", None),
            P("member", "seq", None),
            P("member", "seq", None),
            P("member", None),
            P("member", None),
            P("member", None, None),
        ),
        out_specs=(P("member", "seq", None), P("seq", None)),
        check_vma=False,
    )
```

```python
import math

import jax
import jax.numpy as jnp
from jax import lax
from jax.experimental import pallas as pl
from jax.experimental.pallas import tpu as pltpu
from jax.sharding import PartitionSpec as P

QH = 32
KVH = 4
HD = 64
WINDOW = 128
D = 2880
TOK = 384
XN = 4
ZN = 8
MEM = 4
BQ = 48
BO = 32
NQ = KVH * HD * 2 + QH * HD
CQ = 1024
CO = 1152
CL = 2816

epsilon = 1e-06
softcap = 50.0
rope_base = 10000.0

f32 = jnp.float32
bf16 = jnp.bfloat16
MESH = pl.DeviceIdType.MESH


def mod(a, n):
    return lax.rem(a + n, n)


def kernel(
    hid,
    seg,
    pre_g,
    wq,
    wk,
    wv,
    wo,
    post_g,
    fin_g,
    wj,
    RT,
    LOG,
    WQ,
    WOX,
    WOZ,
    WL,
    SQ,
    SK,
    SV,
    SL,
    HT,
    HID,
    SEG,
    PRE,
    POST,
    FIN,
    WJ,
    NRM,
    A,
    COS,
    SIN,
    Q,
    KV,
    HALO,
    KD,
    VD,
    ATT,
    ATTZ,
    PRJ,
    VS,
    local_sem,
    qx,
    qz,
    qpz,
    qpx,
    ox,
    oz,
    opz,
    opx,
    q_shared,
    ox_shared,
    oz_shared,
    send_sem,
    halo_send,
    halo_recv,
    vs_send,
    vs_recv,
):
    me = lax.axis_index("seq")
    mem = lax.axis_index("member")
    c = lax.rem(me, 2)
    x = lax.rem(me // 2, XN)
    z = me // (2 * XN)
    s = 1 - 2 * c

    def seq_of(zz, xx, cc):
        return (zz * XN + xx) * 2 + cc

    x_f = seq_of(z, mod(x + s, XN), c)
    x_b = seq_of(z, mod(x - s, XN), c)
    z_f = seq_of(mod(z + s, ZN), x, c)
    z_b = seq_of(mod(z - s, ZN), x, c)
    partner = seq_of(z, x, 1 - c)
    after = mod(me + 1, 64)
    before = mod(me - 1, 64)
    far = jnp.where(c == 0, before, after)

    def local(i, src, dst):
        return pltpu.make_async_copy(src, dst, local_sem.at[i])

    own_x = pl.ds(pl.multiple_of(me * BO, BO), BO)
    own_z = pl.ds(pl.multiple_of(((x * ZN + z) * 2 + c) * BO, BO), BO)
    loads = [
        local(0, wk, SK),
        local(1, wv, SV),
        local(2, wq, SQ),
        local(3, hid, HT),
        local(4, wo.at[:, pl.ds(0, CO)], WOX.at[own_x, :]),
        local(5, wo.at[:, pl.ds(CO, CL - CO)], WOZ.at[own_z, :]),
        local(6, pre_g, PRE),
        local(7, seg, SEG),
        local(8, post_g, POST),
        local(9, fin_g, FIN),
        local(10, wj, WJ),
        local(11, wo.at[:, pl.ds(CL, D - CL)], SL),
    ]
    for load in (*loads[:3], loads[11], *loads[3:11]):
        load.start()

    barrier = pltpu.get_barrier_semaphore()
    for peer in (x_f, x_b, z_f, z_b, partner, far):
        pl.semaphore_signal(barrier, inc=1, device_id={"seq": peer}, device_id_type=MESH)
    for delta in (1, 2, 3):
        pl.semaphore_signal(
            barrier, inc=1, device_id={"member": mod(mem + delta, MEM)}, device_id_type=MESH
        )
    loads[11].wait()
    last = SL[...].astype(f32)
    last = jnp.concatenate([last[:16], last[16:]], axis=1)
    last = jnp.concatenate([last[r : r + 1] for r in range(16)], axis=1).astype(bf16)
    own_q = pl.ds(pl.multiple_of(me * BQ, BQ), BQ)
    for load, stage, first, width in ((0, SK, 0, 256), (1, SV, 256, 256), (2, SQ, 512, 2048)):
        loads[load].wait()
        if stage is SQ:
            below = [last, jnp.zeros((2, width), bf16)]
        else:
            below = [jnp.zeros((3, width), bf16)]
        padded = jnp.concatenate([stage[...], *below], axis=0)
        WQ[own_q, pl.ds(first, width)] = padded
    pl.semaphore_wait(barrier, 9)

    def z_order(i):
        return mod(z + s * ((i + 1) // 2) * (1 - 2 * lax.rem(i, 2)), ZN)

    def x_order(i):
        return mod(x + s * ((i + 1) // 2) * (1 - 2 * lax.rem(i, 2)), XN)

    class Gather:
        def __init__(self, number, rows, bufs, shared, rx, rz, pz, px):
            self.number, self.rows, self.bufs, self.shared = number, rows, bufs, shared
            self.rx, self.rz, self.pz, self.px = rx, rz, pz, px

        def block(self, part, zz, xx):
            buf, columns, z_major = self.bufs[part]
            place = seq_of(zz, xx, c) if z_major else (xx * ZN + zz) * 2 + c
            return buf.at[pl.ds(pl.multiple_of(place * self.rows, self.rows), self.rows), columns]

        def copy(self, part, zz, xx, recv, peer):
            ref = self.block(part, zz, xx)
            return pltpu.make_async_remote_copy(
                src_ref=ref,
                dst_ref=ref,
                send_sem=send_sem.at[self.number + part],
                recv_sem=recv,
                device_id={"seq": peer},
                device_id_type=MESH,
            )

        def send(self, part, zz, xx, recv, peer):
            self.copy(part, zz, xx, recv, peer).start()

        def wait(self, part, zz, xx, recv):
            self.copy(part, zz, xx, recv, partner).wait_recv()

        def share(self, part, zz, xx):
            self.send(part, zz, xx, self.shared[part](zz, xx), partner)

        def begin(self):
            self.send(0, z, x, self.rx.at[0], x_f)
            self.send(0, z, x, self.rx.at[1], x_b)
            self.send(1, z, x, self.pz.at[0], z_f)
            self.send(1, z, x, self.pz.at[1], z_b)
            self.send(1, z, x, self.px.at[0], x_f)
            self.send(1, z, x, self.px.at[16], x_b)
            self.send(0, z, x, self.rz.at[0], z_f)
            self.send(0, z, x, self.rz.at[16], z_b)
            self.share(0, z, x)
            self.share(1, z, x)

        def first(self, a):
            zz = z_order(a + 1)
            self.wait(1, zz, x, self.pz.at[a])

            @pl.when(a < 5)
            def _():
                onward = seq_of(mod(z + s * (1 - 2 * lax.rem(a, 2)), ZN), x, c)
                self.send(1, zz, x, self.pz.at[a + 2], onward)

            self.send(1, zz, x, self.px.at[a + 1], x_f)
            self.send(1, zz, x, self.px.at[a + 17], x_b)
            self.share(1, zz, x)

            @pl.when(a < 3)
            def _():
                xx = x_order(a + 1)
                self.wait(0, z, xx, self.rx.at[a])

                @pl.when(a == 0)
                def _():
                    self.send(0, z, xx, self.rx.at[2], x_f)

                self.send(0, z, xx, self.rz.at[a + 1], z_f)
                self.send(0, z, xx, self.rz.at[a + 17], z_b)
                self.share(0, z, xx)

        def second(self, r):
            odd = lax.rem(r, 2)

            @pl.when(r < 12)
            def _():
                xj = x_order(lax.rem(r, 4))
                k = 1 + r // 4
                zf = mod(z - s * k, ZN)
                self.wait(0, zf, xj, self.rz.at[r])

                @pl.when((r < 8) | (odd == 0))
                def _():
                    self.send(0, zf, xj, self.rz.at[r + 4], z_f)

                self.share(0, zf, xj)
                zb = mod(z + s * k, ZN)
                self.wait(0, zb, xj, self.rz.at[r + 16])

                @pl.when(r < 8)
                def _():
                    self.send(0, zb, xj, self.rz.at[r + 20], z_b)

                @pl.when((r >= 8) & (odd == 1))
                def _():
                    self.send(0, zb, xj, self.rz.at[r + 4], z_b)

                self.share(0, zb, xj)

            @pl.when(r >= 12)
            def _():
                for n in range(2):
                    j = 2 * (r - 12) + n
                    zz, xj = mod(z + 4, ZN), x_order(j)
                    self.wait(0, zz, xj, self.rz.at[12 + j])
                    self.share(0, zz, xj)

            @pl.when(r < 8)
            def _():
                zz = z_order(r)
                xf = mod(x - s, XN)
                self.wait(1, zz, xf, self.px.at[r])

                @pl.when(odd == 0)
                def _():
                    self.send(1, zz, xf, self.px.at[r + 8], x_f)

                self.share(1, zz, xf)
                xb = mod(x + s, XN)
                self.wait(1, zz, xb, self.px.at[r + 16])

                @pl.when(odd == 1)
                def _():
                    self.send(1, zz, xb, self.px.at[r + 8], x_b)

                self.share(1, zz, xb)

            @pl.when((r >= 8) & (r < 12))
            def _():
                for n in range(2):
                    i = 2 * (r - 8) + n
                    zz, xx = z_order(i), mod(x + 2, XN)
                    self.wait(1, zz, xx, self.px.at[8 + i])
                    self.share(1, zz, xx)

        def drain(self):
            for part in range(2):
                buf, columns, _ = self.bufs[part]
                sent = buf.at[pl.ds(0, 63 * self.rows), columns]
                pltpu.make_async_copy(sent, sent, send_sem.at[self.number + part]).wait()

    def arrived(sem, ref):
        pltpu.make_async_copy(ref, ref, sem).wait()

    gq = Gather(
        0,
        BQ,
        ((WQ, pl.ds(0, CQ), True), (WQ, pl.ds(CQ, NQ - CQ), True)),
        (lambda zz, xx: q_shared.at[0], lambda zz, xx: q_shared.at[0]),
        qx,
        qz,
        qpz,
        qpx,
    )
    go = Gather(
        2,
        BO,
        ((WOX, slice(None), True), (WOZ, slice(None), False)),
        (lambda zz, xx: ox_shared.at[zz], lambda zz, xx: oz_shared.at[xx]),
        ox,
        oz,
        opz,
        opx,
    )

    gq.begin()

    lane = lax.broadcasted_iota(jnp.int32, (1, 128), 1)
    low_half = lax.rem(lane, 64) < 32
    first_head = lane < 64
    index = lax.rem(lane, 32).astype(f32)
    frequency = jnp.exp(index * (-2.0 * math.log(rope_base) / HD))
    sign = jnp.where(low_half, -1.0, 1.0)

    @pl.loop(0, 3)
    def _(i):
        rows = pl.ds(pl.multiple_of(i * 128, 128), 128)
        position = me * TOK + i * 128 + lax.broadcasted_iota(jnp.int32, (128, 128), 0)
        angle = position.astype(f32) * frequency
        COS[rows, :] = jnp.cos(angle)
        SIN[rows, :] = jnp.sin(angle) * sign

    loads[3].wait()

    @pl.loop(0, 7)
    def _(i):
        for k in range(3):
            features = pl.ds(pl.multiple_of(i * 384 + k * 128, 128), 128)
            HID[:, features] = jnp.transpose(HT[features, :])
        gq.first(i)

    HID[:, pl.ds(2688, 128)] = jnp.transpose(HT[pl.ds(2688, 128), :])
    HID[:, pl.ds(2816, 64)] = jnp.transpose(HT[pl.ds(2816, 64), :])

    loads[6].wait()
    NRM[:, pl.ds(2816, 128)] = jnp.zeros((TOK, 128), bf16)

    @pl.loop(0, 6)
    def _(i):
        rows = pl.ds(pl.multiple_of(i * 64, 64), 64)
        values = HID[rows, :].astype(f32)
        scale = lax.rsqrt(jnp.mean(values * values, axis=-1, keepdims=True) + epsilon)
        NRM[rows, pl.ds(0, D)] = (values * scale * PRE[...]).astype(bf16)
        PRJ[rows, :] = jnp.zeros((64, D), f32)
        gq.second(i)

    @pl.loop(0, 8)
    def _(t):
        start = (t * 360) // 128 * 128
        lead = t * 360 - start
        column = lax.broadcasted_iota(jnp.int32, (1, 384), 1)
        group = jnp.zeros((1, 384), jnp.int32)
        for k in range(1, 8):
            group += jnp.where(column >= 48 * k, 1, 0)
        source = jnp.where(column - 48 * group < 45, column - 3 * group + lead, -1)
        pick = jnp.where(lax.broadcasted_iota(jnp.int32, (512, 384), 0) == source, 1.0, 0.0)
        window = NRM[:, pl.ds(pl.multiple_of(start, 128), 512)]
        moved = jnp.dot(window, pick.astype(bf16), preferred_element_type=f32)
        A[:, pl.ds(pl.multiple_of(t * 384, 384), 384)] = moved.astype(bf16)

        @pl.when(t == 6)
        def _():
            loads[4].wait()
            loads[5].wait()
            go.begin()

        gq.second(t + 6)

    arrived(q_shared.at[0], WQ.at[pl.ds(0, 32 * BQ), :])

    def rotated(half):
        swapped = jnp.where(low_half, pltpu.roll(half, 96, 1), pltpu.roll(half, 32, 1))
        return half * COS[...] + swapped * SIN[...]

    def doubled(pair):
        turned = pltpu.roll(pair, 64, 1)
        return jnp.where(first_head, pair, turned), jnp.where(first_head, turned, pair)

    def project(tile):
        columns = pl.ds(pl.multiple_of(tile * 256, 256), 256)
        return jnp.dot(A[...], WQ[:, columns], preferred_element_type=f32)

    own_rows = pl.ds(WINDOW, TOK)
    keys = project(0)
    for p in range(2):
        pair = rotated(keys[:, 128 * p : 128 * p + 128]).astype(bf16)
        KV[:, pl.ds(128 * p, 128)] = pair
        for q, both in enumerate(doubled(pair.astype(f32))):
            KD[own_rows, pl.ds(128 * (2 * p + q), 128)] = both.astype(bf16)
    vals = project(1)
    for p in range(2):
        pair = vals[:, 128 * p : 128 * p + 128].astype(bf16)
        KV[:, pl.ds(256 + 128 * p, 128)] = pair
        for q, both in enumerate(doubled(pair.astype(f32))):
            VD[own_rows, pl.ds(128 * (2 * p + q), 128)] = both.astype(bf16)

    halo = pltpu.make_async_remote_copy(
        src_ref=KV.at[pl.ds(TOK - WINDOW, WINDOW), :],
        dst_ref=HALO,
        send_sem=halo_send,
        recv_sem=halo_recv,
        device_id={"seq": after},
        device_id_type=MESH,
    )

    def query_tile(i):
        tile = project(i + 2)
        for p in range(2):
            half = rotated(tile[:, 128 * p : 128 * p + 128]) * (1.0 / math.sqrt(HD))
            Q[:, pl.ds(pl.multiple_of(i * 256 + 128 * p, 128), 128)] = half.astype(bf16)

        @pl.when((i == 3) | (i == 6))
        def _():
            go.first(i // 3)

    @pl.loop(0, 1)
    def _(i):
        query_tile(i)

    halo.start()
    go.first(0)

    @pl.loop(1, 8)
    def _(i):
        query_tile(i)

    loads[7].wait()
    ones = jnp.ones((2 * WINDOW, 128), bf16)
    keep_a = jnp.where(first_head, 1.0, 0.0).astype(bf16)
    keep_b = jnp.where(first_head, 0.0, 1.0).astype(bf16)
    q_index = lax.broadcasted_iota(jnp.int32, (WINDOW, WINDOW), 0)
    k_index = lax.broadcasted_iota(jnp.int32, (WINDOW, WINDOW), 1)

    def attend(i):
        block = lax.rem(i // 4 + 1, 3)
        head = lax.rem(i, 4)
        row = me * 3 + block
        seg_own = jnp.broadcast_to(SEG[pl.ds(row, 1), :], (WINDOW, WINDOW))
        seg_old = jnp.broadcast_to(SEG[pl.ds(jnp.maximum(row - 1, 0), 1), :], (WINDOW, WINDOW))
        seg_query = jnp.transpose(seg_own)
        old = (seg_query == seg_old) & (k_index > q_index) & (row > 0)
        new = (seg_query == seg_own) & (k_index <= q_index)
        allowed = jnp.concatenate(
            [jnp.where(old, 1.0, 0.0), jnp.where(new, 1.0, 0.0)], axis=1
        ).astype(bf16)
        allowed = jnp.concatenate([allowed, allowed], axis=0)
        q_rows = pl.ds(pl.multiple_of(block * 128, 128), 128)
        k_rows = pl.ds(pl.multiple_of(block * 128, 128), 256)
        k_cols = pl.ds(pl.multiple_of(head * 128, 128), 128)
        kd = KD[k_rows, k_cols]
        vd = jnp.concatenate([VD[k_rows, k_cols], ones], axis=1)
        mixed = []
        for p in range(4):
            cols = pl.ds(pl.multiple_of(head * 512 + 128 * p, 128), 128)
            pair = Q[q_rows, cols]
            stacked = jnp.concatenate([pair * keep_a, pair * keep_b], axis=0)
            scores = lax.dot_general(
                stacked, kd, (((1,), (1,)), ((), ())), preferred_element_type=f32
            )
            weights = jnp.exp(softcap * jnp.tanh(scores * (1.0 / softcap))).astype(bf16) * allowed
            both = jnp.dot(weights, vd, preferred_element_type=f32)
            both = (both[:, :128] / both[:, 128:]).astype(bf16)
            mixed += [both[:128], both[128:]]
            ATT[q_rows, cols] = jnp.where(first_head, mixed[2 * p], mixed[2 * p + 1])
        for k in range(4):
            cols = pl.ds(pl.multiple_of(k * 512 + head * 128, 128), 128)
            ATTZ[q_rows, cols] = jnp.where(first_head, mixed[k], mixed[k + 4])

    @pl.loop(0, 8)
    def _(i):
        attend(i)

        @pl.when((i == 2) | (i == 5))
        def _():
            go.first(i // 3 + 3)

    go.first(5)
    halo.wait()
    for p in range(2):
        for source, store in ((0, KD), (256, VD)):
            pair = HALO[:, pl.ds(source + 128 * p, 128)].astype(f32)
            for q, both in enumerate(doubled(pair)):
                store[pl.ds(0, WINDOW), pl.ds(128 * (2 * p + q), 128)] = both.astype(bf16)

    @pl.loop(8, 12)
    def _(i):
        attend(i)

    go.first(6)

    def add_z_unit(zz):
        rows = pl.ds(pl.multiple_of(zz * 256, 256), 256)
        arrived(ox_shared.at[zz], WOX.at[pl.ds(0, 4 * BO), :])
        PRJ[:, pl.ds(0, CO)] += jnp.dot(ATT[:, rows], WOX[rows, :], preferred_element_type=f32)

    def add_x_unit(xx):
        rows = pl.ds(pl.multiple_of(xx * 512, 512), 512)
        arrived(oz_shared.at[xx], WOZ.at[pl.ds(0, 8 * BO), :])
        PRJ[:, pl.ds(CO, CL - CO)] += jnp.dot(
            ATTZ[:, rows], WOZ[rows, :], preferred_element_type=f32
        )

    def unpack_last(d):
        rows = pl.ds(pl.multiple_of(d * BQ + 32, 16), 16)
        packed = WQ[rows, pl.ds(512, 2048)].astype(f32)[13:14]
        packed = jnp.concatenate([packed[:, 128 * r : 128 * r + 128] for r in range(16)], axis=0)
        low = jnp.where(first_head, packed, 0.0)
        high = jnp.where(first_head, 0.0, packed)
        WL[pl.ds(pl.multiple_of(d * BO, 16), 16), :] = low.astype(bf16)
        WL[pl.ds(pl.multiple_of(d * BO + 16, 16), 16), :] = high.astype(bf16)

    def add_last():
        both = jnp.dot(ATT[...], WL[...], preferred_element_type=f32)
        PRJ[:, pl.ds(CL, D - CL)] = (both + pltpu.roll(both, 64, 1))[:, : D - CL]

    @pl.loop(0, 14)
    def _(r):
        go.second(r)

        @pl.when((r == 2) | (r == 3))
        def _():
            @pl.loop(0, 8)
            def _(k):
                for j in range(4):
                    unpack_last((r - 2) * 32 + k * 4 + j)

        @pl.when(r == 6)
        def _():
            add_last()

        @pl.when((r == 1) | (r == 4) | (r == 5) | (r == 8) | (r == 9) | (r >= 12))
        def _():
            add_z_unit(z_order(jnp.where(r == 1, 0, jnp.where(r < 6, r - 3, jnp.where(r < 10, r - 5, r - 7)))))

        @pl.when((r == 0) | (r == 10) | (r == 11))
        def _():
            add_x_unit(x_order(jnp.where(r == 0, 0, r - 9)))

    add_z_unit(z_order(7))
    add_x_unit(x_order(3))

    for load in loads[8:11]:
        load.wait()

    def verdict_copy(delta, block):
        rows = pl.ds(pl.multiple_of(block * 128, 128), 128)
        ref = VS.at[mem, rows, :]
        return pltpu.make_async_remote_copy(
            src_ref=ref,
            dst_ref=ref,
            send_sem=vs_send,
            recv_sem=vs_recv.at[(delta - 1) * 3 + block],
            device_id={"member": mod(mem + delta, MEM)},
            device_id_type=MESH,
        )

    def turn(block, first, count):
        tokens = pl.ds(pl.multiple_of(block * 128, 128), 128)
        for k in range(first, first + count):
            features = pl.ds(128 * k, 128 if k < 22 else 64)
            RT[features, tokens] = jnp.transpose(NRM[tokens, features])

    @pl.loop(0, 3)
    def _(i):
        for h in range(2):
            rows = pl.ds(pl.multiple_of(i * 128 + 64 * h, 64), 64)
            projected = PRJ[rows, :]
            scale = lax.rsqrt(jnp.mean(projected * projected, axis=-1, keepdims=True) + epsilon)
            updated = (HID[rows, :].astype(f32) + projected * scale * POST[...]).astype(bf16)
            NRM[rows, pl.ds(0, D)] = updated
            values = updated.astype(f32)
            scale = lax.rsqrt(jnp.mean(values * values, axis=-1, keepdims=True) + epsilon)
            closing = (values * scale * FIN[...]).astype(bf16)
            verdict = jnp.dot(closing, WJ[...], preferred_element_type=f32)
            VS[mem, rows, :] = verdict.astype(bf16)
        turn(i, 0, 8)
        for delta in (2, 1, 3):
            verdict_copy(delta, i).start()
        turn(i, 8, 15)

    gq.drain()
    go.drain()
    for block in range(3):
        for delta in (1, 2, 3):
            verdict_copy(delta, block).wait_recv()
        rows = pl.ds(block * 128, 128)
        total = VS[0, rows, :].astype(f32) + VS[1, rows, :].astype(f32)
        total = total + VS[2, rows, :].astype(f32) + VS[3, rows, :].astype(f32)
        LOG[rows, :] = total * 0.25
    sent = WQ.at[pl.ds(0, 9 * 128), pl.ds(0, 128)]
    arrived(vs_send, sent)


def body(
    hidden, segments, pre_gain, w_query, w_key, w_value, w_output, post_gain, final_gain, w_judge
):
    dma = pltpu.SemaphoreType.DMA
    vmem = pltpu.VMEM
    any_spec = pl.BlockSpec(memory_space=pl.ANY)
    vmem_spec = pl.BlockSpec(memory_space=pltpu.VMEM)
    gather_sems = [dma((3,)), dma((28,)), dma((7,)), dma((24,))]
    updated, logits = pl.pallas_call(
        kernel,
        out_shape=(
            vmem((D, TOK), bf16),
            vmem((TOK, 128), f32),
        ),
        in_specs=[any_spec] * 10,
        out_specs=(vmem_spec, vmem_spec),
        scratch_shapes=[
            vmem((64 * BQ, NQ), bf16),
            vmem((64 * BO, CO), bf16),
            vmem((64 * BO, CL - CO), bf16),
            vmem((64 * BO, 128), bf16),
            vmem((45, 2048), bf16),
            vmem((45, 256), bf16),
            vmem((45, 256), bf16),
            vmem((BO, D - CL), bf16),
            vmem((D, TOK), bf16),
            vmem((TOK, D), bf16),
            vmem((192, 128), jnp.int32),
            vmem((1, D), f32),
            vmem((1, D), f32),
            vmem((1, D), f32),
            vmem((D, 128), bf16),
            vmem((TOK, 2944), bf16),
            vmem((TOK, 64 * BQ), bf16),
            vmem((TOK, 128), f32),
            vmem((TOK, 128), f32),
            vmem((TOK, QH * HD), bf16),
            vmem((TOK, 512), bf16),
            vmem((WINDOW, 512), bf16),
            vmem((WINDOW + TOK, 512), bf16),
            vmem((WINDOW + TOK, 512), bf16),
            vmem((TOK, QH * HD), bf16),
            vmem((TOK, QH * HD), bf16),
            vmem((TOK, D), f32),
            vmem((MEM, TOK, 128), bf16),
            dma((12,)),
            *gather_sems,
            *gather_sems,
            dma((1,)),
            dma((ZN,)),
            dma((XN,)),
            dma((4,)),
            dma,
            dma,
            dma,
            dma((9,)),
        ],
        compiler_params=pltpu.CompilerParams(
            collective_id=0, has_side_effects=True, vmem_limit_bytes=60 * 1024 * 1024
        ),
    )(
        hidden[0].T,
        segments.reshape(192, 128),
        pre_gain,
        w_query[0],
        w_key[0],
        w_value[0],
        w_output[0],
        post_gain,
        final_gain,
        w_judge[0],
    )
    return updated.T[None], logits


def solution(mesh):
    return jax.shard_map(
        body,
        mesh=mesh,
        in_specs=(
            P("member", "seq", None),
            P(),
            P("member", None),
            P("member", "seq", None),
            P("member", "seq", None),
            P("member", "seq", None),
            P("member", "seq", None),
            P("member", None),
            P("member", None),
            P("member", None, None),
        ),
        out_specs=(P("member", "seq", None), P("seq", None)),
        check_vma=False,
    )
```

```python
import math

import jax
import jax.numpy as jnp
from jax import lax
from jax.experimental import pallas as pl
from jax.experimental.pallas import tpu as pltpu
from jax.sharding import PartitionSpec as P

QH = 32
KVH = 4
HD = 64
WINDOW = 128
D = 2880
TOK = 384
XN = 4
ZN = 8
MEM = 4
BQ = 48
BO = 32
NQ = KVH * HD * 2 + QH * HD
CQ = 1024
CO = 896
CL = 2816

epsilon = 1e-06
softcap = 50.0
rope_base = 10000.0

f32 = jnp.float32
bf16 = jnp.bfloat16
MESH = pl.DeviceIdType.MESH


def mod(a, n):
    return lax.rem(a + n, n)


def kernel(
    hid,
    seg,
    pre_g,
    wq,
    wk,
    wv,
    wo,
    post_g,
    fin_g,
    wj,
    RT,
    LOG,
    WQ,
    WOX,
    WOZ,
    WL,
    SQ,
    SK,
    SV,
    SL,
    HT,
    HID,
    SEG,
    PRE,
    POST,
    FIN,
    WJ,
    NRM,
    A,
    COS,
    SIN,
    Q,
    KV,
    HALO,
    KD,
    VD,
    ATT,
    ATTZ,
    PRJ,
    VS,
    local_sem,
    qx,
    qz,
    qpz,
    qpx,
    ox,
    oz,
    opz,
    opx,
    q_shared,
    ox_shared,
    oz_shared,
    send_sem,
    halo_send,
    halo_recv,
    vs_send,
    vs_recv,
):
    me = lax.axis_index("seq")
    mem = lax.axis_index("member")
    c = lax.rem(me, 2)
    x = lax.rem(me // 2, XN)
    z = me // (2 * XN)
    s = 1 - 2 * c

    def seq_of(zz, xx, cc):
        return (zz * XN + xx) * 2 + cc

    x_f = seq_of(z, mod(x + s, XN), c)
    x_b = seq_of(z, mod(x - s, XN), c)
    z_f = seq_of(mod(z + s, ZN), x, c)
    z_b = seq_of(mod(z - s, ZN), x, c)
    partner = seq_of(z, x, 1 - c)
    after = mod(me + 1, 64)
    before = mod(me - 1, 64)
    far = jnp.where(c == 0, before, after)

    def local(i, src, dst):
        return pltpu.make_async_copy(src, dst, local_sem.at[i])

    own_x = pl.ds(pl.multiple_of(me * BO, BO), BO)
    own_z = pl.ds(pl.multiple_of(((x * ZN + z) * 2 + c) * BO, BO), BO)
    loads = [
        local(0, wk, SK),
        local(1, wv, SV),
        local(2, wq, SQ),
        local(3, hid, HT),
        local(4, wo.at[:, pl.ds(0, CO)], WOX.at[own_x, :]),
        local(5, wo.at[:, pl.ds(CO, CL - CO)], WOZ.at[own_z, :]),
        local(6, pre_g, PRE),
        local(7, seg, SEG),
        local(8, post_g, POST),
        local(9, fin_g, FIN),
        local(10, wj, WJ),
        local(11, wo.at[:, pl.ds(CL, D - CL)], SL),
    ]
    for load in (*loads[:3], loads[11]):
        load.start()

    barrier = pltpu.get_barrier_semaphore()
    for peer in (x_f, x_b, z_f, z_b, partner, far):
        pl.semaphore_signal(barrier, inc=1, device_id={"seq": peer}, device_id_type=MESH)
    for delta in (1, 2, 3):
        pl.semaphore_signal(
            barrier, inc=1, device_id={"member": mod(mem + delta, MEM)}, device_id_type=MESH
        )
    for load in loads[3:11]:
        load.start()

    loads[11].wait()
    last = SL[...].astype(f32)
    last = jnp.concatenate([last[:16], last[16:]], axis=1)
    last = jnp.concatenate([last[r : r + 1] for r in range(16)], axis=1).astype(bf16)
    own_q = pl.ds(pl.multiple_of(me * BQ, BQ), BQ)
    for load, stage, first, width in ((0, SK, 0, 256), (1, SV, 256, 256), (2, SQ, 512, 2048)):
        loads[load].wait()
        if stage is SQ:
            below = [last, jnp.zeros((2, width), bf16)]
        else:
            below = [jnp.zeros((3, width), bf16)]
        padded = jnp.concatenate([stage[...], *below], axis=0)
        WQ[own_q, pl.ds(first, width)] = padded
    pl.semaphore_wait(barrier, 9)

    def z_order(i):
        return mod(z + s * ((i + 1) // 2) * (1 - 2 * lax.rem(i, 2)), ZN)

    def x_order(i):
        return mod(x + s * ((i + 1) // 2) * (1 - 2 * lax.rem(i, 2)), XN)

    class Gather:
        def __init__(self, number, rows, bufs, shared, rx, rz, pz, px):
            self.number, self.rows, self.bufs, self.shared = number, rows, bufs, shared
            self.rx, self.rz, self.pz, self.px = rx, rz, pz, px

        def block(self, part, zz, xx):
            buf, columns, z_major = self.bufs[part]
            place = seq_of(zz, xx, c) if z_major else (xx * ZN + zz) * 2 + c
            return buf.at[pl.ds(pl.multiple_of(place * self.rows, self.rows), self.rows), columns]

        def copy(self, part, zz, xx, recv, peer):
            ref = self.block(part, zz, xx)
            return pltpu.make_async_remote_copy(
                src_ref=ref,
                dst_ref=ref,
                send_sem=send_sem.at[self.number + part],
                recv_sem=recv,
                device_id={"seq": peer},
                device_id_type=MESH,
            )

        def send(self, part, zz, xx, recv, peer):
            self.copy(part, zz, xx, recv, peer).start()

        def wait(self, part, zz, xx, recv):
            self.copy(part, zz, xx, recv, partner).wait_recv()

        def share(self, part, zz, xx):
            self.send(part, zz, xx, self.shared[part](zz, xx), partner)

        def begin(self):
            self.send(0, z, x, self.rx.at[0], x_f)
            self.send(0, z, x, self.rx.at[1], x_b)
            self.send(1, z, x, self.pz.at[0], z_f)
            self.send(1, z, x, self.pz.at[1], z_b)
            self.send(1, z, x, self.px.at[0], x_f)
            self.send(1, z, x, self.px.at[16], x_b)
            self.send(0, z, x, self.rz.at[0], z_f)
            self.send(0, z, x, self.rz.at[16], z_b)
            self.share(0, z, x)
            self.share(1, z, x)

        def first(self, a):
            zz = z_order(a + 1)
            self.wait(1, zz, x, self.pz.at[a])

            @pl.when(a < 5)
            def _():
                onward = seq_of(mod(z + s * (1 - 2 * lax.rem(a, 2)), ZN), x, c)
                self.send(1, zz, x, self.pz.at[a + 2], onward)

            self.send(1, zz, x, self.px.at[a + 1], x_f)
            self.send(1, zz, x, self.px.at[a + 17], x_b)
            self.share(1, zz, x)

            @pl.when(a < 3)
            def _():
                xx = x_order(a + 1)
                self.wait(0, z, xx, self.rx.at[a])

                @pl.when(a == 0)
                def _():
                    self.send(0, z, xx, self.rx.at[2], x_f)

                self.send(0, z, xx, self.rz.at[a + 1], z_f)
                self.send(0, z, xx, self.rz.at[a + 17], z_b)
                self.share(0, z, xx)

        def second(self, r):
            odd = lax.rem(r, 2)

            @pl.when(r < 12)
            def _():
                xj = x_order(lax.rem(r, 4))
                k = 1 + r // 4
                zf = mod(z - s * k, ZN)
                self.wait(0, zf, xj, self.rz.at[r])

                @pl.when((r < 8) | (odd == 0))
                def _():
                    self.send(0, zf, xj, self.rz.at[r + 4], z_f)

                self.share(0, zf, xj)
                zb = mod(z + s * k, ZN)
                self.wait(0, zb, xj, self.rz.at[r + 16])

                @pl.when(r < 8)
                def _():
                    self.send(0, zb, xj, self.rz.at[r + 20], z_b)

                @pl.when((r >= 8) & (odd == 1))
                def _():
                    self.send(0, zb, xj, self.rz.at[r + 4], z_b)

                self.share(0, zb, xj)

            @pl.when(r >= 12)
            def _():
                for n in range(2):
                    j = 2 * (r - 12) + n
                    zz, xj = mod(z + 4, ZN), x_order(j)
                    self.wait(0, zz, xj, self.rz.at[12 + j])
                    self.share(0, zz, xj)

            @pl.when(r < 8)
            def _():
                zz = z_order(r)
                xf = mod(x - s, XN)
                self.wait(1, zz, xf, self.px.at[r])

                @pl.when(odd == 0)
                def _():
                    self.send(1, zz, xf, self.px.at[r + 8], x_f)

                self.share(1, zz, xf)
                xb = mod(x + s, XN)
                self.wait(1, zz, xb, self.px.at[r + 16])

                @pl.when(odd == 1)
                def _():
                    self.send(1, zz, xb, self.px.at[r + 8], x_b)

                self.share(1, zz, xb)

            @pl.when((r >= 8) & (r < 12))
            def _():
                for n in range(2):
                    i = 2 * (r - 8) + n
                    zz, xx = z_order(i), mod(x + 2, XN)
                    self.wait(1, zz, xx, self.px.at[8 + i])
                    self.share(1, zz, xx)

        def drain(self):
            for part in range(2):
                buf, columns, _ = self.bufs[part]
                sent = buf.at[pl.ds(0, 63 * self.rows), columns]
                pltpu.make_async_copy(sent, sent, send_sem.at[self.number + part]).wait()

    def arrived(sem, ref):
        pltpu.make_async_copy(ref, ref, sem).wait()

    gq = Gather(
        0,
        BQ,
        ((WQ, pl.ds(0, CQ), True), (WQ, pl.ds(CQ, NQ - CQ), True)),
        (lambda zz, xx: q_shared.at[0], lambda zz, xx: q_shared.at[0]),
        qx,
        qz,
        qpz,
        qpx,
    )
    go = Gather(
        2,
        BO,
        ((WOX, slice(None), True), (WOZ, slice(None), False)),
        (lambda zz, xx: ox_shared.at[zz], lambda zz, xx: oz_shared.at[xx]),
        ox,
        oz,
        opz,
        opx,
    )

    gq.begin()

    lane = lax.broadcasted_iota(jnp.int32, (1, 128), 1)
    low_half = lax.rem(lane, 64) < 32
    first_head = lane < 64
    index = lax.rem(lane, 32).astype(f32)
    frequency = jnp.exp(index * (-2.0 * math.log(rope_base) / HD))
    sign = jnp.where(low_half, -1.0, 1.0)

    @pl.loop(0, 3)
    def _(i):
        rows = pl.ds(pl.multiple_of(i * 128, 128), 128)
        position = me * TOK + i * 128 + lax.broadcasted_iota(jnp.int32, (128, 128), 0)
        angle = position.astype(f32) * frequency
        COS[rows, :] = jnp.cos(angle)
        SIN[rows, :] = jnp.sin(angle) * sign

    loads[3].wait()

    @pl.loop(0, 7)
    def _(i):
        for k in range(3):
            features = pl.ds(pl.multiple_of(i * 384 + k * 128, 128), 128)
            HID[:, features] = jnp.transpose(HT[features, :])
        gq.first(i)

    HID[:, pl.ds(2688, 128)] = jnp.transpose(HT[pl.ds(2688, 128), :])
    HID[:, pl.ds(2816, 64)] = jnp.transpose(HT[pl.ds(2816, 64), :])

    loads[6].wait()
    NRM[:, pl.ds(2816, 128)] = jnp.zeros((TOK, 128), bf16)

    @pl.loop(0, 6)
    def _(i):
        rows = pl.ds(pl.multiple_of(i * 64, 64), 64)
        values = HID[rows, :].astype(f32)
        scale = lax.rsqrt(jnp.mean(values * values, axis=-1, keepdims=True) + epsilon)
        NRM[rows, pl.ds(0, D)] = (values * scale * PRE[...]).astype(bf16)
        PRJ[rows, :] = jnp.zeros((64, D), f32)
        gq.second(i)

    @pl.loop(0, 8)
    def _(t):
        start = (t * 360) // 128 * 128
        lead = t * 360 - start
        column = lax.broadcasted_iota(jnp.int32, (1, 384), 1)
        group = jnp.zeros((1, 384), jnp.int32)
        for k in range(1, 8):
            group += jnp.where(column >= 48 * k, 1, 0)
        source = jnp.where(column - 48 * group < 45, column - 3 * group + lead, -1)
        pick = jnp.where(lax.broadcasted_iota(jnp.int32, (512, 384), 0) == source, 1.0, 0.0)
        window = NRM[:, pl.ds(pl.multiple_of(start, 128), 512)]
        moved = jnp.dot(window, pick.astype(bf16), preferred_element_type=f32)
        A[:, pl.ds(pl.multiple_of(t * 384, 384), 384)] = moved.astype(bf16)

        @pl.when(t == 6)
        def _():
            loads[4].wait()
            loads[5].wait()
            go.begin()

        gq.second(t + 6)

    arrived(q_shared.at[0], WQ.at[pl.ds(0, 32 * BQ), :])

    def rotated(half):
        swapped = jnp.where(low_half, pltpu.roll(half, 96, 1), pltpu.roll(half, 32, 1))
        return half * COS[...] + swapped * SIN[...]

    def doubled(pair):
        turned = pltpu.roll(pair, 64, 1)
        return jnp.where(first_head, pair, turned), jnp.where(first_head, turned, pair)

    def project(tile):
        columns = pl.ds(pl.multiple_of(tile * 256, 256), 256)
        return jnp.dot(A[...], WQ[:, columns], preferred_element_type=f32)

    own_rows = pl.ds(WINDOW, TOK)
    keys = project(0)
    for p in range(2):
        pair = rotated(keys[:, 128 * p : 128 * p + 128]).astype(bf16)
        KV[:, pl.ds(128 * p, 128)] = pair
        for q, both in enumerate(doubled(pair.astype(f32))):
            KD[own_rows, pl.ds(128 * (2 * p + q), 128)] = both.astype(bf16)
    vals = project(1)
    for p in range(2):
        pair = vals[:, 128 * p : 128 * p + 128].astype(bf16)
        KV[:, pl.ds(256 + 128 * p, 128)] = pair
        for q, both in enumerate(doubled(pair.astype(f32))):
            VD[own_rows, pl.ds(128 * (2 * p + q), 128)] = both.astype(bf16)

    halo = pltpu.make_async_remote_copy(
        src_ref=KV.at[pl.ds(TOK - WINDOW, WINDOW), :],
        dst_ref=HALO,
        send_sem=halo_send,
        recv_sem=halo_recv,
        device_id={"seq": after},
        device_id_type=MESH,
    )

    def query_tile(i):
        tile = project(i + 2)
        for p in range(2):
            half = rotated(tile[:, 128 * p : 128 * p + 128]) * (1.0 / math.sqrt(HD))
            Q[:, pl.ds(pl.multiple_of(i * 256 + 128 * p, 128), 128)] = half.astype(bf16)

        @pl.when((i == 3) | (i == 6))
        def _():
            go.first(i // 3)

    @pl.loop(0, 1)
    def _(i):
        query_tile(i)

    halo.start()
    go.first(0)

    @pl.loop(1, 8)
    def _(i):
        query_tile(i)

    loads[7].wait()
    ones = jnp.ones((2 * WINDOW, 128), bf16)
    keep_a = jnp.where(first_head, 1.0, 0.0).astype(bf16)
    keep_b = jnp.where(first_head, 0.0, 1.0).astype(bf16)
    q_index = lax.broadcasted_iota(jnp.int32, (WINDOW, WINDOW), 0)
    k_index = lax.broadcasted_iota(jnp.int32, (WINDOW, WINDOW), 1)

    def attend(i):
        block = lax.rem(i // 4 + 1, 3)
        head = lax.rem(i, 4)
        row = me * 3 + block
        seg_own = jnp.broadcast_to(SEG[pl.ds(row, 1), :], (WINDOW, WINDOW))
        seg_old = jnp.broadcast_to(SEG[pl.ds(jnp.maximum(row - 1, 0), 1), :], (WINDOW, WINDOW))
        seg_query = jnp.transpose(seg_own)
        old = (seg_query == seg_old) & (k_index > q_index) & (row > 0)
        new = (seg_query == seg_own) & (k_index <= q_index)
        allowed = jnp.concatenate(
            [jnp.where(old, 1.0, 0.0), jnp.where(new, 1.0, 0.0)], axis=1
        ).astype(bf16)
        allowed = jnp.concatenate([allowed, allowed], axis=0)
        q_rows = pl.ds(pl.multiple_of(block * 128, 128), 128)
        k_rows = pl.ds(pl.multiple_of(block * 128, 128), 256)
        k_cols = pl.ds(pl.multiple_of(head * 128, 128), 128)
        kd = KD[k_rows, k_cols]
        vd = jnp.concatenate([VD[k_rows, k_cols], ones], axis=1)
        mixed = []
        for p in range(4):
            cols = pl.ds(pl.multiple_of(head * 512 + 128 * p, 128), 128)
            pair = Q[q_rows, cols]
            stacked = jnp.concatenate([pair * keep_a, pair * keep_b], axis=0)
            scores = lax.dot_general(
                stacked, kd, (((1,), (1,)), ((), ())), preferred_element_type=f32
            )
            weights = jnp.exp(softcap * jnp.tanh(scores * (1.0 / softcap))).astype(bf16) * allowed
            both = jnp.dot(weights, vd, preferred_element_type=f32)
            both = (both[:, :128] / both[:, 128:]).astype(bf16)
            mixed += [both[:128], both[128:]]
            ATT[q_rows, cols] = jnp.where(first_head, mixed[2 * p], mixed[2 * p + 1])
        for k in range(4):
            cols = pl.ds(pl.multiple_of(k * 512 + head * 128, 128), 128)
            ATTZ[q_rows, cols] = jnp.where(first_head, mixed[k], mixed[k + 4])

    @pl.loop(0, 8)
    def _(i):
        attend(i)

        @pl.when((i == 2) | (i == 5))
        def _():
            go.first(i // 3 + 3)

    go.first(5)
    halo.wait()
    for p in range(2):
        for source, store in ((0, KD), (256, VD)):
            pair = HALO[:, pl.ds(source + 128 * p, 128)].astype(f32)
            for q, both in enumerate(doubled(pair)):
                store[pl.ds(0, WINDOW), pl.ds(128 * (2 * p + q), 128)] = both.astype(bf16)

    @pl.loop(8, 12)
    def _(i):
        attend(i)

    go.first(6)

    def add_z_unit(zz):
        rows = pl.ds(pl.multiple_of(zz * 256, 256), 256)
        arrived(ox_shared.at[zz], WOX.at[pl.ds(0, 4 * BO), :])
        PRJ[:, pl.ds(0, CO)] += jnp.dot(ATT[:, rows], WOX[rows, :], preferred_element_type=f32)

    def add_x_unit(xx):
        rows = pl.ds(pl.multiple_of(xx * 512, 512), 512)
        arrived(oz_shared.at[xx], WOZ.at[pl.ds(0, 8 * BO), :])
        PRJ[:, pl.ds(CO, CL - CO)] += jnp.dot(
            ATTZ[:, rows], WOZ[rows, :], preferred_element_type=f32
        )

    def unpack_last(d):
        rows = pl.ds(pl.multiple_of(d * BQ + 32, 16), 16)
        packed = WQ[rows, pl.ds(512, 2048)].astype(f32)[13:14]
        packed = jnp.concatenate([packed[:, 128 * r : 128 * r + 128] for r in range(16)], axis=0)
        low = jnp.where(first_head, packed, 0.0)
        high = jnp.where(first_head, 0.0, packed)
        WL[pl.ds(pl.multiple_of(d * BO, 16), 16), :] = low.astype(bf16)
        WL[pl.ds(pl.multiple_of(d * BO + 16, 16), 16), :] = high.astype(bf16)

    def add_last():
        both = jnp.dot(ATT[...], WL[...], preferred_element_type=f32)
        PRJ[:, pl.ds(CL, D - CL)] = (both + pltpu.roll(both, 64, 1))[:, : D - CL]

    @pl.loop(0, 14)
    def _(r):
        go.second(r)

        @pl.when((r == 2) | (r == 3))
        def _():
            @pl.loop(0, 8)
            def _(k):
                for j in range(4):
                    unpack_last((r - 2) * 32 + k * 4 + j)

        @pl.when(r == 6)
        def _():
            add_last()

        @pl.when((r == 1) | (r == 4) | (r == 5) | (r >= 10))
        def _():
            add_z_unit(z_order(jnp.where(r == 1, 0, jnp.where(r < 6, r - 3, r - 7))))

        @pl.when((r == 0) | (r == 8) | (r == 9))
        def _():
            add_x_unit(x_order(jnp.where(r == 0, 0, r - 7)))

    add_x_unit(x_order(3))
    add_z_unit(z_order(7))

    for load in loads[8:11]:
        load.wait()

    def verdict_copy(delta, block):
        rows = pl.ds(pl.multiple_of(block * 128, 128), 128)
        ref = VS.at[mem, rows, :]
        return pltpu.make_async_remote_copy(
            src_ref=ref,
            dst_ref=ref,
            send_sem=vs_send,
            recv_sem=vs_recv.at[(delta - 1) * 3 + block],
            device_id={"member": mod(mem + delta, MEM)},
            device_id_type=MESH,
        )

    def issue(block):
        for delta in (2, 1, 3):
            verdict_copy(delta, block).start()

    def turn(block, first, count):
        tokens = pl.ds(pl.multiple_of(block * 128, 128), 128)
        for k in range(first, first + count):
            features = pl.ds(128 * k, 128 if k < 22 else 64)
            RT[features, tokens] = jnp.transpose(NRM[tokens, features])

    @pl.loop(0, 3)
    def _(i):
        for h in range(2):
            rows = pl.ds(pl.multiple_of(i * 128 + 64 * h, 64), 64)
            projected = PRJ[rows, :]
            scale = lax.rsqrt(jnp.mean(projected * projected, axis=-1, keepdims=True) + epsilon)
            updated = (HID[rows, :].astype(f32) + projected * scale * POST[...]).astype(bf16)
            NRM[rows, pl.ds(0, D)] = updated
            values = updated.astype(f32)
            scale = lax.rsqrt(jnp.mean(values * values, axis=-1, keepdims=True) + epsilon)
            closing = (values * scale * FIN[...]).astype(bf16)
            verdict = jnp.dot(closing, WJ[...], preferred_element_type=f32)
            VS[mem, rows, :] = verdict.astype(bf16)

        @pl.when(i > 0)
        def _():
            issue(i - 1)

    turn(0, 0, 4)
    issue(2)
    turn(0, 4, 19)

    @pl.loop(1, 3)
    def _(i):
        turn(i, 0, 23)

    gq.drain()
    go.drain()
    for block in range(3):
        for delta in (1, 2, 3):
            verdict_copy(delta, block).wait_recv()
        rows = pl.ds(block * 128, 128)
        total = VS[0, rows, :].astype(f32) + VS[1, rows, :].astype(f32)
        total = total + VS[2, rows, :].astype(f32) + VS[3, rows, :].astype(f32)
        LOG[rows, :] = total * 0.25
    sent = WQ.at[pl.ds(0, 9 * 128), pl.ds(0, 128)]
    arrived(vs_send, sent)


def body(
    hidden, segments, pre_gain, w_query, w_key, w_value, w_output, post_gain, final_gain, w_judge
):
    dma = pltpu.SemaphoreType.DMA
    vmem = pltpu.VMEM
    any_spec = pl.BlockSpec(memory_space=pl.ANY)
    vmem_spec = pl.BlockSpec(memory_space=pltpu.VMEM)
    gather_sems = [dma((3,)), dma((28,)), dma((7,)), dma((24,))]
    updated, logits = pl.pallas_call(
        kernel,
        out_shape=(
            vmem((D, TOK), bf16),
            vmem((TOK, 128), f32),
        ),
        in_specs=[any_spec] * 10,
        out_specs=(vmem_spec, vmem_spec),
        scratch_shapes=[
            vmem((64 * BQ, NQ), bf16),
            vmem((64 * BO, CO), bf16),
            vmem((64 * BO, CL - CO), bf16),
            vmem((64 * BO, 128), bf16),
            vmem((45, 2048), bf16),
            vmem((45, 256), bf16),
            vmem((45, 256), bf16),
            vmem((BO, D - CL), bf16),
            vmem((D, TOK), bf16),
            vmem((TOK, D), bf16),
            vmem((192, 128), jnp.int32),
            vmem((1, D), f32),
            vmem((1, D), f32),
            vmem((1, D), f32),
            vmem((D, 128), bf16),
            vmem((TOK, 2944), bf16),
            vmem((TOK, 64 * BQ), bf16),
            vmem((TOK, 128), f32),
            vmem((TOK, 128), f32),
            vmem((TOK, QH * HD), bf16),
            vmem((TOK, 512), bf16),
            vmem((WINDOW, 512), bf16),
            vmem((WINDOW + TOK, 512), bf16),
            vmem((WINDOW + TOK, 512), bf16),
            vmem((TOK, QH * HD), bf16),
            vmem((TOK, QH * HD), bf16),
            vmem((TOK, D), f32),
            vmem((MEM, TOK, 128), bf16),
            dma((12,)),
            *gather_sems,
            *gather_sems,
            dma((1,)),
            dma((ZN,)),
            dma((XN,)),
            dma((4,)),
            dma,
            dma,
            dma,
            dma((9,)),
        ],
        compiler_params=pltpu.CompilerParams(
            collective_id=0, has_side_effects=True, vmem_limit_bytes=60 * 1024 * 1024
        ),
    )(
        hidden[0].T,
        segments.reshape(192, 128),
        pre_gain,
        w_query[0],
        w_key[0],
        w_value[0],
        w_output[0],
        post_gain,
        final_gain,
        w_judge[0],
    )
    return updated.T[None], logits


def solution(mesh):
    return jax.shard_map(
        body,
        mesh=mesh,
        in_specs=(
            P("member", "seq", None),
            P(),
            P("member", None),
            P("member", "seq", None),
            P("member", "seq", None),
            P("member", "seq", None),
            P("member", "seq", None),
            P("member", None),
            P("member", None),
            P("member", None, None),
        ),
        out_specs=(P("member", "seq", None), P("seq", None)),
        check_vma=False,
    )
```
